256 devices in a mesh: mode: 32 (over z_hi, y, core), ex: 4 (over x), ey: 2 (over z_lo).
Axes of the slice: x: 4, y: 4, z: 8 (z_hi: 4, z_lo: 2; z = z_hi * 2 + z_lo), core: 2. Of those that a mesh axis runs over, the one named last changes fastest.
Arguments:
- stream_speed: float32 [12, 12, 16, 4, 2048], P(None, None, 'ex', 'ey', 'mode'), may hold values from -9 to 9, as said below
- normal_speed: float32 [12, 12, 16, 4, 2048], P(None, None, 'ex', 'ey', 'mode'), may hold values from -9 to 9, as said below
Outputs:
- velocity_modes: float32 [12, 12, 16, 4, 4096], P(None, None, 'ex', 'ey', 'mode')
The draws below stay inside these ranges and needn't reach their ends.
Inputs may be any that keep to these rules, and one draw needn't show every extreme that they name: `stream_speed`: continuous across element faces (shared nodes carry equal values), periodic along the streamwise direction and zero on the walls. `normal_speed`: continuous across element faces (shared nodes carry equal values), periodic along the streamwise direction and zero on the walls.
All inputs are finite; a program needn't handle non-finite values.
Results may differ from the reference program's by a relative error of at most 0.00018.
Values sent between devices are 32-bit elements; how exact they have to be, the bound alone decides.
A program may use at most 128 MiB of HBM per device.

```python
import jax
import jax.numpy as jnp
import numpy as np
from jax import lax

P_SIZE = 11
PL_DEV = 64
SWEEPS = 2
EXT = 16
EYT = 4
PLANES = 2048
MODES = 1024
N_MODE = 32


def continuous_field(key):
    grid_x = P_SIZE * EXT
    grid_y = P_SIZE * EYT + 1
    values_grid = jnp.clip(jax.random.normal(key, (grid_x, grid_y, PLANES), jnp.float32), -6.0, 6.0)
    height_index = jnp.arange(grid_y, dtype=jnp.int32)
    inside = jnp.where((height_index > 0) & (height_index < grid_y - 1), 1.0, 0.0).astype(jnp.float32)
    values_grid = values_grid * inside[None, :, None]
    index_x = (P_SIZE * np.arange(EXT)[None, :] + np.arange(P_SIZE + 1)[:, None]) % grid_x
    index_y = P_SIZE * np.arange(EYT)[None, :] + np.arange(P_SIZE + 1)[:, None]
    gathered = values_grid[index_x]
    gathered = gathered[:, :, index_y]
    return jnp.transpose(gathered, (0, 2, 1, 3, 4))


def draw_stream_speed(key, part):
    return continuous_field(jax.random.fold_in(key, 11))


def draw_normal_speed(key, part):
    return continuous_field(jax.random.fold_in(key, 23))


def setup_inputs(seed: int = 0) -> dict:
    streams_of = jax.random.split(jax.random.key(seed), 3)
    return {
        "stream_speed": draw_stream_speed(jax.random.fold_in(streams_of[2], 71), 0),
        "normal_speed": draw_normal_speed(jax.random.fold_in(streams_of[2], 71), 0),
    }


element_width = 2.0
shift_base = 10.0
span_rate = 0.0125

def legendre_pair(degree, points):
    before = points * 0.0 + 1.0
    current = points.copy()
    for step in range(1, degree):
        upcoming = ((2 * step + 1) * points * current - step * before) / (step + 1)
        before = current
        current = upcoming
    return (current, before)

def legendre_slope(degree, points):
    current, before = legendre_pair(degree, points)
    return (current, degree * (points * current - before) / (points * points - 1.0))

def lobatto_points(order):
    guesses = -np.cos(np.pi * np.arange(1, order) / order)
    for step in range(60):
        current, slope = legendre_slope(order, guesses)
        second = (2.0 * guesses * slope - order * (order + 1) * current) / (1.0 - guesses * guesses)
        guesses = guesses - slope / second
    return guesses

def gauss_rule(count):
    guesses = -np.cos(np.pi * (np.arange(count) + 0.75) / (count + 0.5))
    for step in range(60):
        current, slope = legendre_slope(count, guesses)
        guesses = guesses - current / slope
    current, slope = legendre_slope(count, guesses)
    return (guesses, 2.0 / ((1.0 - guesses * guesses) * slope * slope))

def jacobi_eigen(matrix):
    size_n = matrix.shape[0]
    work = matrix.copy()
    vectors = np.eye(size_n)
    for sweep_number in range(20):
        for first in range(size_n):
            for second in range(first + 1, size_n):
                coupling = work[first, second]
                if abs(coupling) > 1e-300:
                    theta = (work[second, second] - work[first, first]) / (2.0 * coupling)
                    direction = 1.0 if theta >= 0.0 else -1.0
                    tangent = direction / (abs(theta) + np.sqrt(theta * theta + 1.0))
                    cosine = 1.0 / np.sqrt(tangent * tangent + 1.0)
                    sine = tangent * cosine
                    rotation = np.eye(size_n)
                    rotation[first, first] = cosine
                    rotation[second, second] = cosine
                    rotation[first, second] = sine
                    rotation[second, first] = -sine
                    work = rotation.T @ work @ rotation
                    vectors = vectors @ rotation
    diagonal_index = np.arange(size_n)
    return (work[diagonal_index, diagonal_index], vectors)

def extended_basis(stiffness, weights, left_width, centre_width, right_width):
    node_count = weights.shape[0]
    full_count = 3 * node_count - 2
    stiff_full = np.zeros((full_count, full_count))
    mass_full = np.zeros(full_count)
    for position, span_width in enumerate((left_width, centre_width, right_width)):
        if span_width > 0.0:
            first_node = position * (node_count - 1)
            stiff_full[first_node:first_node + node_count, first_node:first_node + node_count] += stiffness * (2.0 / span_width)
            mass_full[first_node:first_node + node_count] += weights * (span_width / 2.0)
    low_index = node_count - 2
    high_index = low_index + node_count + 2
    stiff_ext = stiff_full[low_index:high_index, low_index:high_index].copy()
    mass_ext = mass_full[low_index:high_index].copy()
    frozen_list = []
    if left_width <= 0.0:
        frozen_list += [0, 1]
    if right_width <= 0.0:
        frozen_list += [node_count, node_count + 1]
    for frozen_index in frozen_list:
        stiff_ext[frozen_index, :] = 0.0
        stiff_ext[:, frozen_index] = 0.0
        stiff_ext[frozen_index, frozen_index] = 1.0
        mass_ext[frozen_index] = 1.0
    inverse_root = 1.0 / np.sqrt(mass_ext)
    lambdas, vectors = jacobi_eigen(inverse_root[:, None] * stiff_ext * inverse_root[None, :])
    return (inverse_root[:, None] * vectors, lambdas)

def spectral_tables(order, rows_total):
    inner_points = lobatto_points(order)
    points = np.concatenate([[-1.0], inner_points, [1.0]])
    values, unused_before = legendre_pair(order, points)
    weights = 2.0 / (order * (order + 1) * values ** 2)
    identity = np.eye(order + 1)
    point_gaps = points[:, None] - points[None, :] + identity
    derivative = values[:, None] / (values[None, :] * point_gaps) * (1.0 - identity)
    derivative[0, 0] = -order * (order + 1) / 4.0
    derivative[order, order] = order * (order + 1) / 4.0
    stiffness = derivative.T @ (weights[:, None] * derivative)
    gauss_points, gauss_weights = gauss_rule(3 * (order + 1) // 2)
    offsets = gauss_points[:, None, None] - points[None, None, :]
    numerators = np.prod(np.where(identity[None, :, :] > 0.5, 1.0, offsets), axis=2)
    denominators = np.prod(np.where(identity > 0.5, 1.0, points[:, None] - points[None, :]), axis=1)
    interp = numerators / denominators[None, :]
    heights = 0.6 + 1.4 * np.sin(np.pi * (np.arange(rows_total) + 0.5) / rows_total)
    basis_x, lambdas_x = extended_basis(stiffness, weights, element_width, element_width, element_width)
    basis_rows = []
    lambda_rows = []
    for row_number in range(rows_total):
        below = heights[row_number - 1] if row_number > 0 else 0.0
        above = heights[row_number + 1] if row_number < rows_total - 1 else 0.0
        basis_one, lambda_one = extended_basis(stiffness, weights, below, heights[row_number], above)
        basis_rows.append(basis_one)
        lambda_rows.append(lambda_one)
    return (derivative, interp, gauss_weights, weights, stiffness, basis_x, lambdas_x, np.stack(basis_rows), np.stack(lambda_rows), heights)

def device_tables(order, rows_total):
    return tuple((jnp.asarray(table_item, jnp.float32) for table_item in spectral_tables(order, rows_total)))

def along_first(matrix, field_data):
    return jnp.tensordot(matrix, field_data, axes=(1, 0), precision=lax.Precision.HIGHEST)

def along_second(matrix, field_data):
    return jnp.einsum('bj,ajefk->abefk', matrix, field_data, precision=lax.Precision.HIGHEST)

def along_second_rows(matrices, field_data):
    return jnp.einsum('fbj,ajefk->abefk', matrices, field_data, precision=lax.Precision.HIGHEST)

def lift_fine(interp, field_data):
    return along_second(interp, along_first(interp, field_data))

def advection(stream_speed, normal_speed, derivative, interp, gauss_weights, heights):
    height_col = heights[None, None, None, :, None]
    fine_stream = lift_fine(interp, stream_speed)
    fine_normal = lift_fine(interp, normal_speed)
    quadrature = (gauss_weights[:, None] * gauss_weights[None, :])[:, :, None, None, None]

    def convect(speed_field):
        slope_x = along_first(derivative, speed_field) * (2.0 / element_width)
        slope_y = along_second(derivative, speed_field) * (2.0 / height_col)
        product = fine_stream * lift_fine(interp, slope_x) + fine_normal * lift_fine(interp, slope_y)
        returned = along_first(interp.T, along_second(interp.T, product * quadrature))
        return -returned * (element_width * height_col / 4.0)
    return (convect(stream_speed), convect(normal_speed))

def mode_shifts(first_mode, columns):
    column_index = jnp.arange(columns, dtype=jnp.int32)
    mode_index = first_mode + column_index // 4
    return shift_base + (span_rate * mode_index.astype(jnp.float32)) ** 2

def wall_masks(first_row, rows_local, rows_total, node_count):
    row_index = first_row + jnp.arange(rows_local + 2, dtype=jnp.int32) - 1
    node_index = jnp.arange(node_count, dtype=jnp.int32)
    bottom = (row_index[None, :] == 0) & (node_index[:, None] == 0)
    top = (row_index[None, :] == rows_total - 1) & (node_index[:, None] == node_count - 1)
    keep = jnp.where(bottom | top, 0.0, 1.0).astype(jnp.float32)
    return (keep[None, :, None, :, None], keep[None, :, None, 1:-1, None])

def local_operator(solution, stiffness, weights, heights, shift_values):
    height_col = heights[None, None, None, :, None]
    across = along_first(stiffness, solution) * (2.0 / element_width) * (weights[None, :, None, None, None] * height_col / 2.0)
    upward = along_second(stiffness, solution) * (2.0 / height_col) * (weights[:, None, None, None, None] * element_width / 2.0)
    masses = (weights[:, None] * weights[None, :])[:, :, None, None, None] * (element_width * height_col / 4.0)
    return across + upward + masses * shift_values[None, None, None, None, :] * solution

def assemble_first(field_data):
    last_node = field_data.shape[0] - 1
    empty = jnp.zeros_like(field_data[:, :, :1])
    from_left = jnp.concatenate([empty, field_data[:, :, :-1]], 2)
    from_right = jnp.concatenate([field_data[:, :, 1:], empty], 2)
    return jnp.concatenate([field_data[:1] + from_left[last_node:], field_data[1:last_node], field_data[last_node:] + from_right[:1]], 0)

def assemble_second(field_data):
    last_node = field_data.shape[1] - 1
    empty = jnp.zeros_like(field_data[:, :, :, :1])
    from_below = jnp.concatenate([empty, field_data[:, :, :, :-1]], 3)
    from_above = jnp.concatenate([field_data[:, :, :, 1:], empty], 3)
    return jnp.concatenate([field_data[:, :1] + from_below[:, last_node:], field_data[:, 1:last_node], field_data[:, last_node:] + from_above[:, :1]], 1)

def extend_points(extended):
    node_count = extended.shape[0]
    across = jnp.concatenate([extended[node_count - 2:node_count - 1, :, :-2], extended[:, :, 1:-1], extended[1:2, :, 2:]], 0)
    return jnp.concatenate([across[:, node_count - 2:node_count - 1, :, :, :][:, :, :, :-2], across[:, :, :, 1:-1], across[:, 1:2, :, 2:]], 1)

def fold_back(extended):
    point_count = extended.shape[0]
    blank = jnp.zeros_like(extended[:point_count - 6, :, 1:-1])
    across = extended[1:point_count - 1, :, 1:-1] + jnp.concatenate([extended[point_count - 2:, :, :-2], blank, extended[:2, :, 2:]], 0)
    blank_y = jnp.zeros_like(across[:, :point_count - 6, :, 1:-1])
    return across[:, 1:point_count - 1, :, 1:-1] + jnp.concatenate([across[:, point_count - 2:, :, :-2], blank_y, across[:, :2, :, 2:]], 1)

def smooth_modes(forcing, shift_values, row_tables, wall_ext, wall_own, extend):
    stiffness, weights, basis_x, lambdas_x, basis_y, lambdas_y, heights = row_tables
    denominator = lambdas_x[:, None, None, None, None] + jnp.transpose(lambdas_y)[None, :, None, :, None] + shift_values[None, None, None, None, :]
    basis_y_t = jnp.transpose(basis_y, (0, 2, 1))
    solution = jnp.zeros_like(forcing)
    for sweep_index in range(SWEEPS):
        if sweep_index == 0:
            residual = forcing
        else:
            residual = forcing - local_operator(solution, stiffness, weights, heights, shift_values)
        extended = assemble_second(assemble_first(extend(residual))) * wall_ext
        spread = extend_points(extended)
        spectral = along_second_rows(basis_y_t, along_first(basis_x.T, spread)) / denominator
        local_fix = along_first(basis_x, along_second_rows(basis_y, spectral))
        solution = solution + fold_back(extend(local_fix)) * wall_own
    return solution

def grow_blocks(block_field):
    widened = jnp.concatenate([block_field[:, :, -1:], block_field, block_field[:, :, :1]], 2)
    blank = jnp.zeros_like(widened[:, :, :, :1])
    return jnp.concatenate([blank, widened, blank], 3)

def reference(stream_speed, normal_speed):
    derivative, interp, gauss_weights, weights, stiffness, basis_x, lambdas_x, basis_y, lambdas_y, heights = device_tables(P_SIZE, EYT)

    def to_blocks(field_data):
        return jnp.moveaxis(field_data.reshape(field_data.shape[:4] + (N_MODE, PL_DEV)), 4, 0)

    def from_blocks(field_data):
        moved = jnp.moveaxis(field_data, 0, 4)
        return moved.reshape(moved.shape[:4] + (moved.shape[4] * moved.shape[5],))

    def advect_block(speed_pair):
        return advection(speed_pair[0], speed_pair[1], derivative, interp, gauss_weights, heights)
    weak_x, weak_y = lax.map(advect_block, (to_blocks(stream_speed), to_blocks(normal_speed)))
    weak_x = from_blocks(weak_x)
    weak_y = from_blocks(weak_y)
    spectra_x = jnp.fft.rfft(weak_x, axis=-1)[..., :MODES] / PLANES
    spectra_y = jnp.fft.rfft(weak_y, axis=-1)[..., :MODES] / PLANES
    cosine_part = jnp.stack([jnp.real(spectra_x), jnp.real(spectra_y)], -1)
    sine_part = jnp.stack([jnp.imag(spectra_x), jnp.imag(spectra_y)], -1)
    spectra = jnp.stack([cosine_part, sine_part], -2)
    spectra = spectra.reshape(spectra.shape[:4] + (4 * MODES,)).astype(jnp.float32)
    columns = 4 * MODES // N_MODE
    blocks = jnp.moveaxis(spectra.reshape(spectra.shape[:4] + (N_MODE, columns)), 4, 0)
    wall_ext, wall_own = wall_masks(0, EYT, EYT, P_SIZE + 1)
    row_tables = (stiffness, weights, basis_x, lambdas_x, basis_y, lambdas_y, heights)

    def solve_block(block_pair):
        shift_values = mode_shifts(block_pair[1] * (columns // 4), columns)
        return smooth_modes(block_pair[0], shift_values, row_tables, wall_ext, wall_own, grow_blocks)
    solved = lax.map(solve_block, (blocks, jnp.arange(N_MODE, dtype=jnp.int32)))
    return from_blocks(solved)
```

```python
import functools
import math

import jax
import jax.numpy as jnp
import numpy as np
from jax import lax
from jax.experimental import pallas as pl
from jax.experimental.pallas import tpu as pltpu
from jax.sharding import PartitionSpec as P

P_SIZE = 11
NODES = P_SIZE + 1
FINE = 18
FINE_PAD = 336
ELEMS = 4
ROWS_DEV = 2
ROWS_TOTAL = 4
PLANES = 2048
RANKS = 32
LINE = 24
COLS = 48
GRID = COLS * LINE
FLAT = 1024
EXT_POINTS = NODES + 2
SPECTRAL = ROWS_DEV * EXT_POINTS * 16
WINDOW = EXT_POINTS * LINE
OWN = NODES * LINE

MESH = pl.DeviceIdType.MESH
F32 = jnp.float32
BF16 = jnp.bfloat16

element_width = 2.0
shift_base = 10.0
span_rate = 0.0125


def legendre_pair(degree, points):
    before = points * 0.0 + 1.0
    current = points.copy()
    for step in range(1, degree):
        upcoming = ((2 * step + 1) * points * current - step * before) / (step + 1)
        before = current
        current = upcoming
    return (current, before)


def legendre_slope(degree, points):
    current, before = legendre_pair(degree, points)
    return (current, degree * (points * current - before) / (points * points - 1.0))


def lobatto_points(order):
    guesses = -np.cos(np.pi * np.arange(1, order) / order)
    for step in range(60):
        current, slope = legendre_slope(order, guesses)
        second = (2.0 * guesses * slope - order * (order + 1) * current) / (1.0 - guesses * guesses)
        guesses = guesses - slope / second
    return guesses


def gauss_rule(count):
    guesses = -np.cos(np.pi * (np.arange(count) + 0.75) / (count + 0.5))
    for step in range(60):
        current, slope = legendre_slope(count, guesses)
        guesses = guesses - current / slope
    current, slope = legendre_slope(count, guesses)
    return (guesses, 2.0 / ((1.0 - guesses * guesses) * slope * slope))


def jacobi_eigen(matrix):
    size_n = matrix.shape[0]
    work = matrix.copy()
    vectors = np.eye(size_n)
    for sweep_number in range(20):
        for first in range(size_n):
            for second in range(first + 1, size_n):
                coupling = work[first, second]
                if abs(coupling) > 1e-300:
                    theta = (work[second, second] - work[first, first]) / (2.0 * coupling)
                    direction = 1.0 if theta >= 0.0 else -1.0
                    tangent = direction / (abs(theta) + np.sqrt(theta * theta + 1.0))
                    cosine = 1.0 / np.sqrt(tangent * tangent + 1.0)
                    sine = tangent * cosine
                    rotation = np.eye(size_n)
                    rotation[first, first] = cosine
                    rotation[second, second] = cosine
                    rotation[first, second] = sine
                    rotation[second, first] = -sine
                    work = rotation.T @ work @ rotation
                    vectors = vectors @ rotation
    diagonal_index = np.arange(size_n)
    return (work[diagonal_index, diagonal_index], vectors)


def extended_basis(stiffness, weights, left_width, centre_width, right_width):
    node_count = weights.shape[0]
    full_count = 3 * node_count - 2
    stiff_full = np.zeros((full_count, full_count))
    mass_full = np.zeros(full_count)
    for position, span_width in enumerate((left_width, centre_width, right_width)):
        if span_width > 0.0:
            first_node = position * (node_count - 1)
            stiff_full[
                first_node : first_node + node_count, first_node : first_node + node_count
            ] += stiffness * (2.0 / span_width)
            mass_full[first_node : first_node + node_count] += weights * (span_width / 2.0)
    low_index = node_count - 2
    high_index = low_index + node_count + 2
    stiff_ext = stiff_full[low_index:high_index, low_index:high_index].copy()
    mass_ext = mass_full[low_index:high_index].copy()
    frozen_list = []
    if left_width <= 0.0:
        frozen_list += [0, 1]
    if right_width <= 0.0:
        frozen_list += [node_count, node_count + 1]
    for frozen_index in frozen_list:
        stiff_ext[frozen_index, :] = 0.0
        stiff_ext[:, frozen_index] = 0.0
        stiff_ext[frozen_index, frozen_index] = 1.0
        mass_ext[frozen_index] = 1.0
    inverse_root = 1.0 / np.sqrt(mass_ext)
    lambdas, vectors = jacobi_eigen(inverse_root[:, None] * stiff_ext * inverse_root[None, :])
    return (inverse_root[:, None] * vectors, lambdas)


def spectral_tables(order, rows_total):
    inner_points = lobatto_points(order)
    points = np.concatenate([[-1.0], inner_points, [1.0]])
    values, unused_before = legendre_pair(order, points)
    weights = 2.0 / (order * (order + 1) * values**2)
    identity = np.eye(order + 1)
    point_gaps = points[:, None] - points[None, :] + identity
    derivative = values[:, None] / (values[None, :] * point_gaps) * (1.0 - identity)
    derivative[0, 0] = -order * (order + 1) / 4.0
    derivative[order, order] = order * (order + 1) / 4.0
    stiffness = derivative.T @ (weights[:, None] * derivative)
    gauss_points, gauss_weights = gauss_rule(3 * (order + 1) // 2)
    offsets = gauss_points[:, None, None] - points[None, None, :]
    numerators = np.prod(np.where(identity[None, :, :] > 0.5, 1.0, offsets), axis=2)
    denominators = np.prod(np.where(identity > 0.5, 1.0, points[:, None] - points[None, :]), axis=1)
    interp = numerators / denominators[None, :]
    heights = 0.6 + 1.4 * np.sin(np.pi * (np.arange(rows_total) + 0.5) / rows_total)
    basis_x, lambdas_x = extended_basis(
        stiffness, weights, element_width, element_width, element_width
    )
    basis_rows = []
    lambda_rows = []
    for row_number in range(rows_total):
        below = heights[row_number - 1] if row_number > 0 else 0.0
        above = heights[row_number + 1] if row_number < rows_total - 1 else 0.0
        basis_one, lambda_one = extended_basis(
            stiffness, weights, below, heights[row_number], above
        )
        basis_rows.append(basis_one)
        lambda_rows.append(lambda_one)
    return (
        derivative,
        interp,
        gauss_weights,
        weights,
        stiffness,
        basis_x,
        lambdas_x,
        np.stack(basis_rows),
        np.stack(lambda_rows),
        heights,
    )


def bf16_pair(table):
    high = np.asarray(table, np.float32).astype(BF16)
    low = (np.asarray(table, np.float64) - high.astype(np.float64)).astype(np.float32)
    return high, low.astype(BF16)


def split(value):
    high = value.astype(BF16)
    return high, (value - high.astype(F32)).astype(BF16)


def dot(left, right):
    return jnp.dot(left, right, preferred_element_type=F32)


def dot_rows(left, right):
    return lax.dot_general(left, right, (((1,), (1,)), ((), ())), preferred_element_type=F32)


@functools.cache
def all_tables():
    (derivative, interp, gauss_weights, weights, stiffness, basis_x, lambdas_x, basis_y,
     lambdas_y, heights) = spectral_tables(P_SIZE, ROWS_TOTAL)
    nodes = NODES * NODES
    fine = FINE * FINE
    lift = np.zeros((3, FINE_PAD, nodes))
    lift[0, :fine] = np.kron(interp, interp)
    lift[1, :fine] = np.kron(interp @ derivative * (2.0 / element_width), interp)
    lift[2, :fine] = np.kron(interp, interp @ derivative)
    lift = lift.reshape(3 * FINE_PAD, nodes)
    lift_high, lift_low = bf16_pair(lift)
    lift_cat = np.concatenate([lift_high, lift_high, lift_low], 1)
    back = np.zeros((NODES, LINE, ROWS_DEV, FINE_PAD))
    quad = np.kron(gauss_weights, gauss_weights)
    back_one = -(np.kron(interp.T, interp.T) * quad[None, :]).reshape(NODES, NODES, fine)
    for f in range(ROWS_DEV):
        back[:, P_SIZE * f : P_SIZE * f + NODES, f, :fine] += back_one
    back_high, back_low = bf16_pair(back.reshape(NODES * LINE, ROWS_DEV * FINE_PAD))
    plane = np.arange(64)[None, :]
    fourier = np.zeros((16, 2, 2, 32, 2, 64))
    for rp in range(16):
        for half in range(2):
            r = rp if half == 0 else (32 - rp if rp else 16)
            mode = 32 * np.arange(32)[:, None] + r
            angle = 2.0 * np.pi * ((mode * plane) % PLANES) / PLANES
            cosine, sine = np.cos(angle) / PLANES, np.sin(angle) / PLANES
            if rp == 0:
                fourier[rp, half, 0, :, half] = cosine
                fourier[rp, half, 1, :, half] = -sine
            else:
                sign = 1.0 if half == 0 else -1.0
                fourier[rp, half, 0, :, 0] = cosine
                fourier[rp, half, 0, :, 1] = sign * sine
                fourier[rp, half, 1, :, 0] = -sine
                fourier[rp, half, 1, :, 1] = sign * cosine
    four_high, four_low = bf16_pair(fourier.reshape(16, 128, 128))
    four_cat = np.concatenate([four_high, four_low], 2)
    line_basis = np.zeros((2, ROWS_DEV, LINE, 16))
    line_lambda = np.ones((2, ROWS_DEV, 16))
    line_mass = np.zeros((2, LINE))
    line_stiff = np.zeros((2, LINE, LINE))
    top = P_SIZE * ROWS_TOTAL
    for ey in range(2):
        low = 21 * ey
        for f in range(ROWS_DEV):
            row = ROWS_DEV * ey + f
            line_lambda[ey, f, :EXT_POINTS] = lambdas_y[row]
            for b in range(EXT_POINTS):
                g = P_SIZE * row + b - 1
                if 0 < g < top:
                    line_basis[ey, f, g - low, :EXT_POINTS] = basis_y[row, b]
            for b in range(NODES):
                g = P_SIZE * row + b
                if 0 < g < top:
                    line_mass[ey, g - low] += heights[row] / 2.0 * weights[b]
                    for c in range(NODES):
                        h = P_SIZE * row + c
                        if 0 < h < top:
                            line_stiff[ey, g - low, h - low] += 2.0 / heights[row] * stiffness[b, c]
    ones_line = np.ones(LINE)
    in_x = np.kron(basis_x.T, ones_line[None, :])
    in_y = np.tile(np.transpose(line_basis, (0, 1, 3, 2)), (1, 1, 1, EXT_POINTS))
    out_x = np.tile(np.kron(basis_x, np.ones((1, 16))), (1, ROWS_DEV))
    out_y = np.concatenate(
        [np.tile(line_basis[:, f], (1, 1, EXT_POINTS)) for f in range(ROWS_DEV)], 2)
    eye = np.eye(NODES)
    own_kx = np.kron(stiffness * (2.0 / element_width), ones_line[None, :])
    own_my = np.tile(line_mass[:, :, None] * np.eye(LINE)[None], (1, 1, NODES))
    own_wx = np.kron(np.diag(weights) * (element_width / 2.0), ones_line[None, :])
    own_ky = np.tile(line_stiff, (1, 1, NODES))
    wide = np.ones((1, 1, 128))
    single = dict(
        lift=lift_cat, back_high=back_high, back_low=back_low, fourier=four_cat)
    single.update({name: np.asarray(table, np.float32) for name, table in dict(
        in_x=in_x, in_y=in_y, out_x=out_x, out_y=out_y,
        own_kx=own_kx, own_my=own_my, own_wx=own_wx, own_ky=own_ky,
        mass=line_mass[:, :, None] * wide, lam=line_lambda[..., None] * wide[None]).items()})
    return single, np.asarray(lambdas_x), np.asarray(weights), np.asarray(heights)


def advect_kernel(heights, u_ref, v_ref, lift_ref, high_ref, low_ref, out_ref):
    ey = lax.axis_index("ey")
    lane = lax.broadcasted_iota(jnp.int32, (FINE_PAD, 128), 1)
    first = lane < 64
    products = []
    for f in range(ROWS_DEV):
        columns = []
        for e in range(ELEMS):
            rows = pl.ds(ROWS_DEV * e + f, NODES * NODES, stride=ROWS_DEV * ELEMS)
            columns.append(jnp.concatenate([u_ref[rows, :], v_ref[rows, :]], 1))
        high, low = split(jnp.concatenate(columns, 1))
        fine = dot(lift_ref[...], jnp.concatenate([high, low, high], 0))
        half_height = jnp.where(
            ey == 0, np.float32(heights[f] / 2.0), np.float32(heights[ROWS_DEV + f] / 2.0))
        parts = []
        for e in range(ELEMS):
            block = slice(128 * e, 128 * e + 128)
            speed = fine[:FINE_PAD, block]
            turned = pltpu.roll(speed, 64, 1)
            along = jnp.where(first, speed, turned) * half_height
            across = jnp.where(first, turned, speed)
            parts.append(
                along * fine[FINE_PAD : 2 * FINE_PAD, block] + across * fine[2 * FINE_PAD :, block])
        products.append(jnp.concatenate(parts, 1))
    high, low = split(jnp.concatenate(products, 0))
    weak = dot(high_ref[...], high) + dot(high_ref[...], low) + dot(low_ref[...], high)
    weak = jnp.where(ey == 0, pltpu.roll(weak, OWN - 1, 0), weak)
    for e in range(ELEMS):
        for a in range(NODES):
            if a == P_SIZE and e < ELEMS - 1:
                continue
            value = weak[LINE * a : LINE * a + 22, 128 * e : 128 * e + 128]
            if a == 0 and e > 0:
                value += weak[LINE * P_SIZE : LINE * P_SIZE + 22, 128 * e - 128 : 128 * e]
            x = P_SIZE * e + a
            out_ref[22 * x : 22 * x + 22, :] = value
    out_ref[990:, :] = jnp.zeros((FLAT - 990, 128), F32)


def real_transform(values):
    count = len(values)
    if count == 1:
        return [(values[0], None)]
    if count == 2:
        return [(values[0] + values[1], None), (values[0] - values[1], None)]
    even, odd = real_transform(values[0::2]), real_transform(values[1::2])
    quarter, half = count // 4, count // 2
    result = []
    for r in range(half + 1):
        s = r % half

        def pick(part):
            if s <= quarter:
                return part[s], 1.0
            return part[half - s], -1.0

        (er, ei), es = pick(even)
        (dr, di), ds = pick(odd)
        c, n = math.cos(2 * math.pi * r / count), -math.sin(2 * math.pi * r / count)
        if r == 0:
            result.append((er + dr, None))
        elif r == half:
            result.append((er - dr, None))
        elif 4 * r == count:
            result.append((er, -dr))
        else:
            c, n = np.float32(c), np.float32(n)
            if di is None:
                tr, ti = dr * c, dr * n
            else:
                tr = dr * c - di * (n * np.float32(ds))
                ti = dr * n + di * (c * np.float32(ds))
            result.append((er + tr, ti if ei is None else (ti + ei if es > 0 else ti - ei)))
    return result


def transform_kernel(in_ref, table_ref, out_ref, mid_ref, turn_ref):
    for block in range(4):
        rows = slice(8 * block, 8 * block + 8)
        values = [in_ref[32 * d + 8 * block : 32 * d + 8 * block + 8, :] for d in range(RANKS)]
        found = real_transform(values)
        for r in range(1, 16):
            mid_ref[2 * r, rows, :], mid_ref[2 * r + 1, rows, :] = found[r]
        mid_ref[0, rows, :] = found[0][0]
        mid_ref[1, rows, :] = found[16][0]
    first = lax.broadcasted_iota(jnp.int32, (32, 128), 1) < 64
    for rp in range(16):
        real, imag = mid_ref[2 * rp], mid_ref[2 * rp + 1]
        both = jnp.concatenate(
            [jnp.where(first, real, pltpu.roll(imag, 64, 1)),
             jnp.where(first, pltpu.roll(real, 64, 1), imag)], 0)
        high, low = split(both)
        table = table_ref[rp]
        found = dot_rows(table, jnp.concatenate([high, high], 1)) + dot_rows(table[:, :128], low)
        for half in range(2):
            r = rp if half == 0 else (32 - rp if rp else 16)
            for c in range(2):
                start = 32 * (2 * half + c)
                for k in range(2):
                    turn_ref[pl.ds(4 * r + 2 * c + k, 32, stride=128), :] = found[start : start + 32, :]
    even = lax.broadcasted_iota(jnp.int32, (32, 128), 1) % 2 == 0
    for q in range(RANKS):
        turned = turn_ref[128 * q : 128 * q + 128, :].T
        out_ref[32 * q : 32 * q + 32, :] = jnp.where(even, turned[:32], turned[32:])


def share_kernel(in_ref, out_ref, send_sem, recv_sem):
    me = lax.axis_index("mode")
    barrier = pltpu.get_barrier_semaphore()

    def signal(i, carry):
        pl.semaphore_signal(
            barrier, inc=1, device_id={"mode": lax.rem(me + i, RANKS)}, device_id_type=MESH)
        return carry

    lax.fori_loop(1, RANKS, signal, 0)
    pl.semaphore_wait(barrier, RANKS - 1)

    def copy(i):
        peer = lax.rem(me + i, RANKS)
        return pltpu.make_async_remote_copy(
            src_ref=in_ref.at[pl.ds(pl.multiple_of(32 * peer, 32), 32)],
            dst_ref=out_ref.at[pl.ds(pl.multiple_of(32 * me, 32), 32)],
            send_sem=send_sem.at[i],
            recv_sem=recv_sem.at[i],
            device_id={"mode": peer},
            device_id_type=MESH,
        )

    def start(i, carry):
        copy(i).start()
        return carry

    def finish(i, carry):
        copy(i).wait()
        return carry

    lax.fori_loop(1, RANKS, start, 0)
    mine = pl.ds(pl.multiple_of(32 * me, 32), 32)
    out_ref[mine, :] = in_ref[mine, :]
    lax.fori_loop(1, RANKS, finish, 0)


RESIDUAL = ((1, 44, 45, 0), (21, 22), (1, 0))
CORRECTION = ((0, 45, 44, 1), (22, 21), (0, 1))


def smooth_kernel(
    lambdas_x, weights, flat_ref, in_x, in_y, out_x, out_y, own_kx, own_my, own_wx, own_ky, mass_ref,
    lam_ref, out_ref, inward, outward, local, inverse, raw, field, fix, total, side, line, corner,
    side_in, line_in, corner_in, send_sem, recv_sem):
    ey = lax.axis_index("ey")
    ex = lax.axis_index("ex")
    left, right = lax.rem(ex + 3, 4), lax.rem(ex + 1, 4)
    other = 1 - ey
    low_side = ey == 0
    peers = ({"ex": left}, {"ex": right}, {"ey": other},
             {"ex": left, "ey": other}, {"ex": right, "ey": other})
    barrier = pltpu.get_barrier_semaphore()
    for peer in peers:
        pl.semaphore_signal(barrier, inc=1, device_id=peer, device_id_type=MESH)

    raw[...] = jnp.zeros((GRID, 128), F32)
    for x in range(45):
        raw[LINE * (x + 1) + 1 : LINE * (x + 1) + 23, :] = flat_ref[22 * x : 22 * x + 22, :]

    lane = lax.broadcasted_iota(jnp.int32, (1, 128), 1)
    mode = (lax.axis_index("mode") * 32 + lane // 4).astype(F32)
    shift = shift_base + (np.float32(span_rate) * mode) ** 2
    for f in range(ROWS_DEV):
        for i in range(EXT_POINTS):
            row = 16 * (EXT_POINTS * f + i)
            high, low = split(in_x[i : i + 1, :] * in_y[ey, f])
            inward[0, row : row + 16, :] = high
            inward[1, row : row + 16, :] = low
            inverse[row : row + 16, :] = 1.0 / (lam_ref[ey, f] + (shift + np.float32(lambdas_x[i])))
    high, low = split(jnp.concatenate([out_x[a : a + 1, :] * out_y[ey] for a in range(EXT_POINTS)], 0))
    outward[0], outward[1] = high, low
    high, low = split(jnp.concatenate(
        [own_kx[a : a + 1, :] * own_my[ey] + own_wx[a : a + 1, :] * own_ky[ey] for a in range(NODES)], 0))
    local[0], local[1] = high, low

    pl.semaphore_wait(barrier, 5)

    def exchange(number, grid, kind):
        (to_left, to_right, from_right, from_left), lower, upper = kind
        side[number, 0] = grid[LINE * to_left : LINE * to_left + 48, :]
        side[number, 1] = grid[LINE * to_right : LINE * to_right + 48, :]
        zero = jnp.zeros((4, 128), F32)
        pieces = []
        for step in range(2):
            rows = jnp.where(
                low_side,
                grid[pl.ds(lower[0] + step, COLS, stride=LINE), :],
                grid[pl.ds(upper[0] + step, COLS, stride=LINE), :])
            line[number, step] = rows
            pieces.append(rows)
        for at, column in enumerate((to_left, to_right)):
            corner[number, at] = jnp.concatenate([p[column : column + 2] for p in pieces] + [zero], 0)
        sends = (
            (side.at[number, 0], side_in.at[number, 0]),
            (side.at[number, 1], side_in.at[number, 1]),
            (line.at[number], line_in.at[number]),
            (corner.at[number, 0], corner_in.at[number, 0]),
            (corner.at[number, 1], corner_in.at[number, 1]))
        copies = []
        for at, ((source, target), peer) in enumerate(zip(sends, peers, strict=True)):
            copies.append(pltpu.make_async_remote_copy(
                src_ref=source, dst_ref=target, send_sem=send_sem.at[number, at],
                recv_sem=recv_sem.at[number, at], device_id=peer, device_id_type=MESH))
            copies[-1].start()
        for sent in copies:
            sent.wait()
        grid[LINE * from_right : LINE * from_right + 48, :] += side_in[number, 0]
        grid[LINE * from_left : LINE * from_left + 48, :] += side_in[number, 1]
        zeros = jnp.zeros((COLS, 128), F32)
        for step in range(2):
            rows = [line_in[number, step]]
            for at, column in enumerate((from_right, from_left)):
                piece = corner_in[number, at, 2 * step : 2 * step + 2, :]
                before = [jnp.zeros((column, 128), F32)] if column else []
                rows.append(jnp.concatenate(
                    before + [piece, jnp.zeros((COLS - 2 - column, 128), F32)], 0))
            added = rows[0] + rows[1] + rows[2]
            where_low = pl.ds(lower[1] + step, COLS, stride=LINE)
            where_up = pl.ds(upper[1] + step, COLS, stride=LINE)
            grid[where_low, :] += jnp.where(low_side, added, zeros)
            grid[where_up, :] += jnp.where(low_side, zeros, added)

    def solve(source, target):
        value = jnp.concatenate(
            [source[264 * e : 264 * e + WINDOW, :] for e in range(ELEMS)], 1)
        high, low = split(value)
        modal = dot(inward[0], high) + dot(inward[0], low) + dot(inward[1], high)
        modal = modal * jnp.concatenate([inverse[...]] * ELEMS, 1)
        high, low = split(modal)
        back = dot(outward[0], high) + dot(outward[0], low) + dot(outward[1], high)
        target[...] = jnp.zeros((GRID, 128), F32)
        for e in range(ELEMS):
            target[264 * e : 264 * e + WINDOW, :] += back[:, 128 * e : 128 * e + 128]

    field[...] = raw[...]
    exchange(0, field, RESIDUAL)
    solve(field, total)
    exchange(1, total, CORRECTION)
    value = jnp.concatenate(
        [total[264 * e + LINE : 264 * e + LINE + OWN, :] for e in range(ELEMS)], 1)
    high, low = split(value)
    applied = dot(local[0], high) + dot(local[0], low) + dot(local[1], high)
    coefficient = jnp.concatenate(
        [(np.float32(weights[a] * element_width / 2.0) * shift) * mass_ref[ey] for a in range(NODES)], 0)
    applied = applied + value * jnp.concatenate([coefficient] * ELEMS, 1)
    field[...] = raw[...]
    for e in range(ELEMS):
        field[264 * e + LINE : 264 * e + LINE + OWN, :] -= applied[:, 128 * e : 128 * e + 128]
    exchange(2, field, RESIDUAL)
    solve(field, fix)
    exchange(3, fix, CORRECTION)
    total[...] += fix[...]
    for e in range(ELEMS):
        for f in range(ROWS_DEV):
            for a in range(NODES):
                start = LINE * (P_SIZE * e + 1 + a) + P_SIZE * f
                out_ref[pl.ds(96 * a + 2 * e + f, NODES, stride=8), :] = jnp.where(
                    low_side, total[start : start + NODES, :], total[start + 1 : start + 1 + NODES, :])


def on_device(stream_speed, normal_speed):
    single, lambdas_x, weights, heights = all_tables()
    vmem = pl.BlockSpec(memory_space=pltpu.VMEM)
    flat = jax.ShapeDtypeStruct((FLAT, 128), F32)

    def share(value, number):
        return pl.pallas_call(
            share_kernel,
            out_shape=flat,
            in_specs=[vmem],
            out_specs=vmem,
            scratch_shapes=[pltpu.SemaphoreType.DMA((RANKS,)), pltpu.SemaphoreType.DMA((RANKS,))],
            compiler_params=pltpu.CompilerParams(collective_id=number, has_side_effects=True),
            name=f"share_{number}",
        )(value)

    tables = {name: jnp.asarray(table) for name, table in single.items()}
    weak = pl.pallas_call(
        functools.partial(advect_kernel, heights),
        out_shape=flat,
        in_specs=[vmem] * 5,
        out_specs=vmem,
        name="advect",
    )(stream_speed.reshape(1152, 64), normal_speed.reshape(1152, 64), tables["lift"],
      tables["back_high"], tables["back_low"])
    spectra = pl.pallas_call(
        transform_kernel,
        out_shape=flat,
        in_specs=[vmem] * 2,
        out_specs=vmem,
        scratch_shapes=[pltpu.VMEM((32, 32, 128), F32), pltpu.VMEM((4096, 64), F32)],
        name="transform",
    )(share(weak, 1), tables["fourier"])
    names = ("in_x", "in_y", "out_x", "out_y", "own_kx", "own_my", "own_wx", "own_ky", "mass", "lam")
    grid = pltpu.VMEM((GRID, 128), F32)
    solved = pl.pallas_call(
        functools.partial(smooth_kernel, lambdas_x, weights),
        out_shape=jax.ShapeDtypeStruct((1152, 128), F32),
        in_specs=[vmem] * (1 + len(names)),
        out_specs=vmem,
        scratch_shapes=[
            pltpu.VMEM((2, SPECTRAL, WINDOW), BF16),
            pltpu.VMEM((2, WINDOW, SPECTRAL), BF16),
            pltpu.VMEM((2, OWN, OWN), BF16),
            pltpu.VMEM((SPECTRAL, 128), F32),
            grid, grid, grid, grid,
            pltpu.VMEM((4, 2, 48, 128), F32),
            pltpu.VMEM((4, 2, COLS, 128), F32),
            pltpu.VMEM((4, 2, 8, 128), F32),
            pltpu.VMEM((4, 2, 48, 128), F32),
            pltpu.VMEM((4, 2, COLS, 128), F32),
            pltpu.VMEM((4, 2, 8, 128), F32),
            pltpu.SemaphoreType.DMA((4, 5)),
            pltpu.SemaphoreType.DMA((4, 5)),
        ],
        compiler_params=pltpu.CompilerParams(collective_id=3, has_side_effects=True),
        name="smooth",
    )(share(spectra, 2), *[tables[name] for name in names])
    return solved.reshape(12, 12, 4, 2, 128)


def solution(mesh):
    return jax.shard_map(
        on_device,
        mesh=mesh,
        in_specs=(P(None, None, "ex", "ey", "mode"), P(None, None, "ex", "ey", "mode")),
        out_specs=P(None, None, "ex", "ey", "mode"),
        check_vma=False,
    )
```

```python
import functools
import math

import jax
import jax.numpy as jnp
import numpy as np
from jax import lax
from jax.experimental import pallas as pl
from jax.experimental.pallas import tpu as pltpu
from jax.sharding import PartitionSpec as P

P_SIZE = 11
NODES = P_SIZE + 1
FINE = 18
FINE_PAD = 336
ELEMS = 4
ROWS_DEV = 2
ROWS_TOTAL = 4
PLANES = 2048
RANKS = 32
LINE = 24
COLS = 48
GRID = COLS * LINE
FLAT = 1024
EXT_POINTS = NODES + 2
SPECTRAL = ROWS_DEV * EXT_POINTS * 16
WINDOW = EXT_POINTS * LINE
OWN = NODES * LINE

MESH = pl.DeviceIdType.MESH
F32 = jnp.float32
BF16 = jnp.bfloat16

element_width = 2.0
shift_base = 10.0
span_rate = 0.0125


def legendre_pair(degree, points):
    before = points * 0.0 + 1.0
    current = points.copy()
    for step in range(1, degree):
        upcoming = ((2 * step + 1) * points * current - step * before) / (step + 1)
        before = current
        current = upcoming
    return (current, before)


def legendre_slope(degree, points):
    current, before = legendre_pair(degree, points)
    return (current, degree * (points * current - before) / (points * points - 1.0))


def lobatto_points(order):
    guesses = -np.cos(np.pi * np.arange(1, order) / order)
    for step in range(60):
        current, slope = legendre_slope(order, guesses)
        second = (2.0 * guesses * slope - order * (order + 1) * current) / (1.0 - guesses * guesses)
        guesses = guesses - slope / second
    return guesses


def gauss_rule(count):
    guesses = -np.cos(np.pi * (np.arange(count) + 0.75) / (count + 0.5))
    for step in range(60):
        current, slope = legendre_slope(count, guesses)
        guesses = guesses - current / slope
    current, slope = legendre_slope(count, guesses)
    return (guesses, 2.0 / ((1.0 - guesses * guesses) * slope * slope))


def jacobi_eigen(matrix):
    size_n = matrix.shape[0]
    work = matrix.copy()
    vectors = np.eye(size_n)
    for sweep_number in range(20):
        for first in range(size_n):
            for second in range(first + 1, size_n):
                coupling = work[first, second]
                if abs(coupling) > 1e-300:
                    theta = (work[second, second] - work[first, first]) / (2.0 * coupling)
                    direction = 1.0 if theta >= 0.0 else -1.0
                    tangent = direction / (abs(theta) + np.sqrt(theta * theta + 1.0))
                    cosine = 1.0 / np.sqrt(tangent * tangent + 1.0)
                    sine = tangent * cosine
                    rotation = np.eye(size_n)
                    rotation[first, first] = cosine
                    rotation[second, second] = cosine
                    rotation[first, second] = sine
                    rotation[second, first] = -sine
                    work = rotation.T @ work @ rotation
                    vectors = vectors @ rotation
    diagonal_index = np.arange(size_n)
    return (work[diagonal_index, diagonal_index], vectors)


def extended_basis(stiffness, weights, left_width, centre_width, right_width):
    node_count = weights.shape[0]
    full_count = 3 * node_count - 2
    stiff_full = np.zeros((full_count, full_count))
    mass_full = np.zeros(full_count)
    for position, span_width in enumerate((left_width, centre_width, right_width)):
        if span_width > 0.0:
            first_node = position * (node_count - 1)
            stiff_full[
                first_node : first_node + node_count, first_node : first_node + node_count
            ] += stiffness * (2.0 / span_width)
            mass_full[first_node : first_node + node_count] += weights * (span_width / 2.0)
    low_index = node_count - 2
    high_index = low_index + node_count + 2
    stiff_ext = stiff_full[low_index:high_index, low_index:high_index].copy()
    mass_ext = mass_full[low_index:high_index].copy()
    frozen_list = []
    if left_width <= 0.0:
        frozen_list += [0, 1]
    if right_width <= 0.0:
        frozen_list += [node_count, node_count + 1]
    for frozen_index in frozen_list:
        stiff_ext[frozen_index, :] = 0.0
        stiff_ext[:, frozen_index] = 0.0
        stiff_ext[frozen_index, frozen_index] = 1.0
        mass_ext[frozen_index] = 1.0
    inverse_root = 1.0 / np.sqrt(mass_ext)
    lambdas, vectors = jacobi_eigen(inverse_root[:, None] * stiff_ext * inverse_root[None, :])
    return (inverse_root[:, None] * vectors, lambdas)


def spectral_tables(order, rows_total):
    inner_points = lobatto_points(order)
    points = np.concatenate([[-1.0], inner_points, [1.0]])
    values, unused_before = legendre_pair(order, points)
    weights = 2.0 / (order * (order + 1) * values**2)
    identity = np.eye(order + 1)
    point_gaps = points[:, None] - points[None, :] + identity
    derivative = values[:, None] / (values[None, :] * point_gaps) * (1.0 - identity)
    derivative[0, 0] = -order * (order + 1) / 4.0
    derivative[order, order] = order * (order + 1) / 4.0
    stiffness = derivative.T @ (weights[:, None] * derivative)
    gauss_points, gauss_weights = gauss_rule(3 * (order + 1) // 2)
    offsets = gauss_points[:, None, None] - points[None, None, :]
    numerators = np.prod(np.where(identity[None, :, :] > 0.5, 1.0, offsets), axis=2)
    denominators = np.prod(np.where(identity > 0.5, 1.0, points[:, None] - points[None, :]), axis=1)
    interp = numerators / denominators[None, :]
    heights = 0.6 + 1.4 * np.sin(np.pi * (np.arange(rows_total) + 0.5) / rows_total)
    basis_x, lambdas_x = extended_basis(
        stiffness, weights, element_width, element_width, element_width
    )
    basis_rows = []
    lambda_rows = []
    for row_number in range(rows_total):
        below = heights[row_number - 1] if row_number > 0 else 0.0
        above = heights[row_number + 1] if row_number < rows_total - 1 else 0.0
        basis_one, lambda_one = extended_basis(
            stiffness, weights, below, heights[row_number], above
        )
        basis_rows.append(basis_one)
        lambda_rows.append(lambda_one)
    return (
        derivative,
        interp,
        gauss_weights,
        weights,
        stiffness,
        basis_x,
        lambdas_x,
        np.stack(basis_rows),
        np.stack(lambda_rows),
        heights,
    )


def bf16_pair(table):
    high = np.asarray(table, np.float32).astype(BF16)
    low = (np.asarray(table, np.float64) - high.astype(np.float64)).astype(np.float32)
    return high, low.astype(BF16)


def split(value):
    high = value.astype(BF16)
    return high, (value - high.astype(F32)).astype(BF16)


def dot(left, right):
    return jnp.dot(left, right, preferred_element_type=F32)


def dot_rows(left, right):
    return lax.dot_general(left, right, (((1,), (1,)), ((), ())), preferred_element_type=F32)


@functools.cache
def all_tables():
    (derivative, interp, gauss_weights, weights, stiffness, basis_x, lambdas_x, basis_y,
     lambdas_y, heights) = spectral_tables(P_SIZE, ROWS_TOTAL)
    nodes = NODES * NODES
    fine = FINE * FINE
    lift = np.zeros((3, FINE_PAD, nodes))
    lift[0, :fine] = np.kron(interp, interp)
    lift[1, :fine] = np.kron(interp @ derivative * (2.0 / element_width), interp)
    lift[2, :fine] = np.kron(interp, interp @ derivative)
    lift = lift.reshape(3 * FINE_PAD, nodes)
    lift_high, lift_low = bf16_pair(lift)
    lift_cat = np.concatenate([lift_high, lift_high, lift_low], 1)
    back = np.zeros((NODES, LINE, ROWS_DEV, FINE_PAD))
    quad = np.kron(gauss_weights, gauss_weights)
    back_one = -(np.kron(interp.T, interp.T) * quad[None, :]).reshape(NODES, NODES, fine)
    for f in range(ROWS_DEV):
        back[:, P_SIZE * f : P_SIZE * f + NODES, f, :fine] += back_one
    back_high, back_low = bf16_pair(back.reshape(NODES * LINE, ROWS_DEV * FINE_PAD))
    plane = np.arange(64)[None, :]
    angle = 2.0 * np.pi * ((np.arange(32)[:, None] * plane) % 64) / 64.0
    wave = np.tile(np.stack([np.cos(angle), np.sin(angle)]), (1, 1, 2))
    twist = np.zeros((16, 4, 2, 2, 64))
    for rp in range(16):
        for half in range(2):
            r = rp if half == 0 else (32 - rp if rp else 16)
            turn = 2.0 * np.pi * r * np.arange(64) / PLANES
            cosine = np.stack([np.cos(turn), -np.sin(turn)]) / PLANES
            sine = np.stack([np.sin(turn), np.cos(turn)]) / PLANES
            if rp == 0:
                twist[rp, 2 * half, :, half] = cosine
                twist[rp, 2 * half + 1, :, half] = -sine
            else:
                sign = 1.0 if half == 0 else -1.0
                twist[rp, 2 * half, :, 0] = cosine
                twist[rp, 2 * half, :, 1] = sign * sine
                twist[rp, 2 * half + 1, :, 0] = -sine
                twist[rp, 2 * half + 1, :, 1] = sign * cosine
    twist = twist.reshape(16, 8, 128)
    line_basis = np.zeros((2, ROWS_DEV, LINE, 16))
    line_lambda = np.ones((2, ROWS_DEV, 16))
    line_mass = np.zeros((2, LINE))
    line_stiff = np.zeros((2, LINE, LINE))
    top = P_SIZE * ROWS_TOTAL
    for ey in range(2):
        low = 21 * ey
        for f in range(ROWS_DEV):
            row = ROWS_DEV * ey + f
            line_lambda[ey, f, :EXT_POINTS] = lambdas_y[row]
            for b in range(EXT_POINTS):
                g = P_SIZE * row + b - 1
                if 0 < g < top:
                    line_basis[ey, f, g - low, :EXT_POINTS] = basis_y[row, b]
            for b in range(NODES):
                g = P_SIZE * row + b
                if 0 < g < top:
                    line_mass[ey, g - low] += heights[row] / 2.0 * weights[b]
                    for c in range(NODES):
                        h = P_SIZE * row + c
                        if 0 < h < top:
                            line_stiff[ey, g - low, h - low] += 2.0 / heights[row] * stiffness[b, c]
    ones_line = np.ones(LINE)
    in_x = np.kron(basis_x.T, ones_line[None, :])
    in_y = np.tile(np.transpose(line_basis, (0, 1, 3, 2)), (1, 1, 1, EXT_POINTS))
    out_x = np.tile(np.kron(basis_x, np.ones((1, 16))), (1, ROWS_DEV))
    out_y = np.concatenate(
        [np.tile(line_basis[:, f], (1, 1, EXT_POINTS)) for f in range(ROWS_DEV)], 2)
    eye = np.eye(NODES)
    own_kx = np.kron(stiffness * (2.0 / element_width), ones_line[None, :])
    own_my = np.tile(line_mass[:, :, None] * np.eye(LINE)[None], (1, 1, NODES))
    own_wx = np.kron(np.diag(weights) * (element_width / 2.0), ones_line[None, :])
    own_ky = np.tile(line_stiff, (1, 1, NODES))
    wide = np.ones((1, 1, 128))
    single = dict(lift=lift_cat, back_high=back_high, back_low=back_low)
    single.update({name: np.asarray(table, np.float32) for name, table in dict(
        wave=wave, twist=twist,
        in_x=in_x, in_y=in_y, out_x=out_x, out_y=out_y,
        own_kx=own_kx, own_my=own_my, own_wx=own_wx, own_ky=own_ky,
        mass=line_mass[:, :, None] * wide, lam=line_lambda[..., None] * wide[None]).items()})
    return single, np.asarray(lambdas_x), np.asarray(weights), np.asarray(heights)


def real_transform(values):
    count = len(values)
    if count == 1:
        return [(values[0], None)]
    if count == 2:
        return [(values[0] + values[1], None), (values[0] - values[1], None)]
    even, odd = real_transform(values[0::2]), real_transform(values[1::2])
    quarter, half = count // 4, count // 2
    result = []
    for r in range(half + 1):
        s = r % half

        def pick(part):
            if s <= quarter:
                return part[s], 1.0
            return part[half - s], -1.0

        (er, ei), es = pick(even)
        (dr, di), ds = pick(odd)
        c, n = math.cos(2 * math.pi * r / count), -math.sin(2 * math.pi * r / count)
        if r == 0:
            result.append((er + dr, None))
        elif r == half:
            result.append((er - dr, None))
        elif 4 * r == count:
            result.append((er, -dr))
        else:
            c, n = np.float32(c), np.float32(n)
            if di is None:
                tr, ti = dr * c, dr * n
            else:
                tr = dr * c - di * (n * np.float32(ds))
                ti = dr * n + di * (c * np.float32(ds))
            result.append((er + tr, ti if ei is None else (ti + ei if es > 0 else ti - ei)))
    return result


def flat_row(x):
    return 22 * x if x < 22 else FLAT // 2 + 22 * (x - 22)


RESIDUAL = ((1, 44, 45, 0), (21, 22), (1, 0))
CORRECTION = ((0, 45, 44, 1), (22, 21), (0, 1))
TABLES = ("back_high", "back_low", "wave", "twist", "in_x", "in_y", "out_x", "out_y", "own_kx", "own_my", "own_wx",
          "own_ky", "mass", "lam")


def step_kernel(lambdas_x, weights, heights, u_ref, v_ref, lift_ref, *refs):
    count = len(TABLES)
    sources, out_ref, refs = refs[:count], refs[count], refs[count + 1 :]
    held, refs = dict(zip(TABLES, refs[:count], strict=True)), refs[count:]
    (weak_out, weak_in, modal_out, modal_in, mid_ref, turn_ref, fourier, inward, outward, local, inverse,
     raw, field, fix, total, side, line, corner, side_in, line_in, corner_in,
     table_sem, share_send, share_recv, send_sem, recv_sem) = refs
    me = lax.axis_index("mode")
    ey = lax.axis_index("ey")
    ex = lax.axis_index("ex")
    low_side = ey == 0
    my_z, my_y, my_c = me // 8, lax.rem(me // 2, 4), lax.rem(me, 2)

    def rank(dz, group):
        dy, dc = group // 2, lax.rem(group, 2)
        return 8 * lax.rem(my_z + dz, 4) + 2 * lax.rem(my_y + dy, 4) + lax.rem(my_c + dc, 2)

    def each_rank(act):
        for dz in (2, 1, 3):
            act(dz, jnp.int32(0))

        def body(group, carry):
            for dz in (2, 1, 3, 0):
                act(dz, group)
            return carry

        lax.fori_loop(1, 8, body, 0)

    loads = [pltpu.make_async_copy(source, held[name], table_sem.at[at])
             for at, (name, source) in enumerate(zip(TABLES, sources, strict=True))]
    for load in loads:
        load.start()

    left, right, other = lax.rem(ex + 3, 4), lax.rem(ex + 1, 4), 1 - ey
    peers = ({"ex": left, "ey": other}, {"ex": right, "ey": other}, {"ey": other}, {"ex": left}, {"ex": right})
    barrier = pltpu.get_barrier_semaphore()
    each_rank(lambda dz, group: pl.semaphore_signal(
        barrier, inc=1, device_id={"mode": rank(dz, group)}, device_id_type=MESH))
    for peer in peers:
        pl.semaphore_signal(barrier, inc=1, device_id=peer, device_id_type=MESH)

    def advect(half):
        first = lax.broadcasted_iota(jnp.int32, (FINE_PAD, 128), 1) < 64
        products = []
        for f in range(ROWS_DEV):
            columns = []
            for e in (2 * half, 2 * half + 1):
                rows = pl.ds(ROWS_DEV * e + f, NODES * NODES, stride=ROWS_DEV * ELEMS)
                columns.append(jnp.concatenate([u_ref[rows, :], v_ref[rows, :]], 1))
            high, low = split(jnp.concatenate(columns, 1))
            fine = dot(lift_ref[...], jnp.concatenate([high, low, high], 0))
            half_height = jnp.where(
                low_side, np.float32(heights[f] / 2.0), np.float32(heights[ROWS_DEV + f] / 2.0))
            parts = []
            for e in range(2):
                block = slice(128 * e, 128 * e + 128)
                speed = fine[:FINE_PAD, block]
                turned = pltpu.roll(speed, 64, 1)
                along = jnp.where(first, speed, turned) * half_height
                across = jnp.where(first, turned, speed)
                parts.append(
                    along * fine[FINE_PAD : 2 * FINE_PAD, block] + across * fine[2 * FINE_PAD :, block])
            products.append(jnp.concatenate(parts, 1))
        high, low = split(jnp.concatenate(products, 0))
        if half == 0:
            loads[0].wait()
            loads[1].wait()
        back_high, back_low = held["back_high"], held["back_low"]
        weak = dot(back_high[...], high) + dot(back_high[...], low) + dot(back_low[...], high)
        return jnp.where(low_side, pltpu.roll(weak, OWN - 1, 0), weak)

    def store_weak(half, weak, carried):
        for e in range(2):
            for a in range(NODES):
                x = P_SIZE * (2 * half + e) + a
                if a == P_SIZE and x < 44:
                    continue
                value = weak[LINE * a : LINE * a + 22, 128 * e : 128 * e + 128]
                if a == 0 and e == 1:
                    value += weak[LINE * P_SIZE : LINE * P_SIZE + 22, :128]
                if a == 0 and e == 0 and half == 1:
                    value += carried
                weak_out[flat_row(x) : flat_row(x) + 22, :] = value
        spare = (484, 512) if half == 0 else (1018, 1024)
        weak_out[spare[0] : spare[1], :] = jnp.zeros((spare[1] - spare[0], 128), F32)
        return weak[LINE * P_SIZE : LINE * P_SIZE + 22, 128:]

    def share(stage, half):
        source, target = ((weak_out, weak_in), (modal_out, modal_in))[stage]
        base, number = FLAT // 2 * half, 2 * stage + half

        def copy(dz, group):
            at = 8 * dz + group
            peer = rank(dz, group)
            return pltpu.make_async_remote_copy(
                src_ref=source.at[pl.ds(pl.multiple_of(base + 16 * peer, 16), 16)],
                dst_ref=target.at[pl.ds(pl.multiple_of(base + 16 * me, 16), 16)],
                send_sem=share_send.at[number, at],
                recv_sem=share_recv.at[number, at],
                device_id={"mode": peer},
                device_id_type=MESH,
            )

        return copy

    def send(stage, half):
        copy = share(stage, half)
        each_rank(lambda dz, group: copy(dz, group).start())
        source, target = ((weak_out, weak_in), (modal_out, modal_in))[stage]
        mine = pl.ds(pl.multiple_of(FLAT // 2 * half + 16 * me, 16), 16)
        target[mine, :] = source[mine, :]

    def receive(stage, half):
        copy = share(stage, half)
        each_rank(lambda dz, group: copy(dz, group).wait_recv())

    def transform(half):
        base = FLAT // 2 * half
        for block in range(2):
            rows = slice(8 * block, 8 * block + 8)
            starts = [base + 16 * d + 8 * block for d in range(RANKS)]
            found = real_transform([weak_in[s : s + 8, :] for s in starts])
            for r in range(1, 16):
                mid_ref[2 * r, rows, :], mid_ref[2 * r + 1, rows, :] = found[r]
            mid_ref[0, rows, :] = found[0][0]
            mid_ref[1, rows, :] = found[16][0]
        first = lax.broadcasted_iota(jnp.int32, (16, 128), 1) < 64
        for rp in range(16):
            real, imag = mid_ref[2 * rp], mid_ref[2 * rp + 1]
            both = jnp.concatenate(
                [jnp.where(first, real, pltpu.roll(imag, 64, 1)),
                 jnp.where(first, pltpu.roll(real, 64, 1), imag)], 0)
            high, low = split(both)
            table = fourier[rp]
            found = dot_rows(table, jnp.concatenate([high, high], 1)) + dot_rows(table[:, :128], low)
            for at in range(2):
                r = rp if at == 0 else (32 - rp if rp else 16)
                for c in range(2):
                    start = 32 * (2 * at + c)
                    for k in range(2):
                        turn_ref[pl.ds(4 * r + 2 * c + k, 32, stride=128), :] = found[start : start + 32, :]
        even = lax.broadcasted_iota(jnp.int32, (16, 128), 1) % 2 == 0
        for q in range(RANKS):
            turned = turn_ref[128 * q : 128 * q + 128, :].T
            modal_out[base + 16 * q : base + 16 * q + 16, :] = jnp.where(even, turned[:16], turned[16:])

    carried = store_weak(0, advect(0), None)
    pl.semaphore_wait(barrier, RANKS - 1 + 5)
    send(0, 0)
    store_weak(1, advect(1), carried)
    send(0, 1)

    for load in loads[2:]:
        load.wait()
    for rp in range(16):
        for at in range(4):
            pair = held["twist"][rp, 2 * at : 2 * at + 2, :]
            high, low = split(held["wave"][0] * pair[:1] + held["wave"][1] * pair[1:])
            fourier[rp, 32 * at : 32 * at + 32, :128] = high
            fourier[rp, 32 * at : 32 * at + 32, 128:] = low
    lane = lax.broadcasted_iota(jnp.int32, (1, 128), 1)
    mode = (me * 32 + lane // 4).astype(F32)
    shift = shift_base + (np.float32(span_rate) * mode) ** 2
    for f in range(ROWS_DEV):
        for i in range(EXT_POINTS):
            row = 16 * (EXT_POINTS * f + i)
            high, low = split(held["in_x"][i : i + 1, :] * held["in_y"][ey, f])
            inward[0, row : row + 16, :] = high
            inward[1, row : row + 16, :] = low
            inverse[row : row + 16, :] = 1.0 / (held["lam"][ey, f] + (shift + np.float32(lambdas_x[i])))
    high, low = split(jnp.concatenate(
        [held["out_x"][a : a + 1, :] * held["out_y"][ey] for a in range(EXT_POINTS)], 0))
    outward[0], outward[1] = high, low
    high, low = split(jnp.concatenate(
        [held["own_kx"][a : a + 1, :] * held["own_my"][ey] + held["own_wx"][a : a + 1, :] * held["own_ky"][ey]
         for a in range(NODES)], 0))
    local[0], local[1] = high, low
    raw[...] = jnp.zeros((GRID, 128), F32)

    for half in range(2):
        receive(0, half)
        transform(half)
        send(1, half)
    for half in range(2):
        receive(1, half)
        for x in range(22 * half, 22 + 23 * half):
            raw[LINE * (x + 1) + 1 : LINE * (x + 1) + 23, :] = modal_in[flat_row(x) : flat_row(x) + 22, :]

    def exchange(number, grid, kind):
        (to_left, to_right, from_right, from_left), lower, upper = kind
        zero = jnp.zeros((4, 128), F32)
        pieces = []
        for step in range(2):
            rows = jnp.where(
                low_side,
                grid[pl.ds(lower[0] + step, COLS, stride=LINE), :],
                grid[pl.ds(upper[0] + step, COLS, stride=LINE), :])
            line[number, step] = rows
            pieces.append(rows)
        for at, column in enumerate((to_left, to_right)):
            corner[number, at] = jnp.concatenate([p[column : column + 2] for p in pieces] + [zero], 0)
        side[number, 0] = grid[LINE * to_left : LINE * to_left + 48, :]
        side[number, 1] = grid[LINE * to_right : LINE * to_right + 48, :]
        sends = (
            (corner.at[number, 0], corner_in.at[number, 0]),
            (corner.at[number, 1], corner_in.at[number, 1]),
            (line.at[number], line_in.at[number]),
            (side.at[number, 0], side_in.at[number, 0]),
            (side.at[number, 1], side_in.at[number, 1]))
        copies = []
        for at, ((source, target), peer) in enumerate(zip(sends, peers, strict=True)):
            copies.append(pltpu.make_async_remote_copy(
                src_ref=source, dst_ref=target, send_sem=send_sem.at[number, at],
                recv_sem=recv_sem.at[number, at], device_id=peer, device_id_type=MESH))
            copies[-1].start()
        copies[3].wait_recv()
        copies[4].wait_recv()
        grid[LINE * from_right : LINE * from_right + 48, :] += side_in[number, 0]
        grid[LINE * from_left : LINE * from_left + 48, :] += side_in[number, 1]
        copies[2].wait_recv()
        copies[0].wait_recv()
        copies[1].wait_recv()
        zeros = jnp.zeros((COLS, 128), F32)
        for step in range(2):
            rows = [line_in[number, step]]
            for at, column in enumerate((from_right, from_left)):
                piece = corner_in[number, at, 2 * step : 2 * step + 2, :]
                before = [jnp.zeros((column, 128), F32)] if column else []
                rows.append(jnp.concatenate(
                    before + [piece, jnp.zeros((COLS - 2 - column, 128), F32)], 0))
            added = rows[0] + rows[1] + rows[2]
            where_low = pl.ds(lower[1] + step, COLS, stride=LINE)
            where_up = pl.ds(upper[1] + step, COLS, stride=LINE)
            grid[where_low, :] += jnp.where(low_side, added, zeros)
            grid[where_up, :] += jnp.where(low_side, zeros, added)
        return copies

    def solve(source, target):
        value = jnp.concatenate(
            [source[264 * e : 264 * e + WINDOW, :] for e in range(ELEMS)], 1)
        high, low = split(value)
        modal = dot(inward[0], high) + dot(inward[0], low) + dot(inward[1], high)
        modal = modal * jnp.concatenate([inverse[...]] * ELEMS, 1)
        high, low = split(modal)
        back = dot(outward[0], high) + dot(outward[0], low) + dot(outward[1], high)
        target[...] = jnp.zeros((GRID, 128), F32)
        for e in range(ELEMS):
            target[264 * e : 264 * e + WINDOW, :] += back[:, 128 * e : 128 * e + 128]

    sent = []
    field[...] = raw[...]
    sent += exchange(0, field, RESIDUAL)
    solve(field, total)
    sent += exchange(1, total, CORRECTION)
    value = jnp.concatenate(
        [total[264 * e + LINE : 264 * e + LINE + OWN, :] for e in range(ELEMS)], 1)
    high, low = split(value)
    applied = dot(local[0], high) + dot(local[0], low) + dot(local[1], high)
    coefficient = jnp.concatenate(
        [(np.float32(weights[a] * element_width / 2.0) * shift) * held["mass"][ey] for a in range(NODES)], 0)
    applied = applied + value * jnp.concatenate([coefficient] * ELEMS, 1)
    field[...] = raw[...]
    for e in range(ELEMS):
        field[264 * e + LINE : 264 * e + LINE + OWN, :] -= applied[:, 128 * e : 128 * e + 128]
    sent += exchange(2, field, RESIDUAL)
    solve(field, fix)
    sent += exchange(3, fix, CORRECTION)
    out_ref[...] = total[...] + fix[...]
    for one in sent:
        one.wait_send()
    for stage in range(2):
        for half in range(2):
            copy = share(stage, half)
            each_rank(lambda dz, group, copy=copy: copy(dz, group).wait_send())


def place_kernel(grid_ref, out_ref):
    low_side = lax.axis_index("ey") == 0
    for e in range(ELEMS):
        for f in range(ROWS_DEV):
            for a in range(NODES):
                start = LINE * (P_SIZE * e + 1 + a) + P_SIZE * f
                out_ref[pl.ds(96 * a + 2 * e + f, NODES, stride=8), :] = jnp.where(
                    low_side, grid_ref[start : start + NODES, :], grid_ref[start + 1 : start + 1 + NODES, :])


def on_device(stream_speed, normal_speed):
    single, lambdas_x, weights, heights = all_tables()
    vmem = pl.BlockSpec(memory_space=pltpu.VMEM)
    anywhere = pl.BlockSpec(memory_space=pl.ANY)
    tables = {name: jnp.asarray(table) for name, table in single.items()}
    grid = pltpu.VMEM((GRID, 128), F32)
    flat = pltpu.VMEM((FLAT, 128), F32)
    solved = pl.pallas_call(
        functools.partial(step_kernel, lambdas_x, weights, heights),
        out_shape=jax.ShapeDtypeStruct((GRID, 128), F32),
        in_specs=[vmem] * 3 + [anywhere] * len(TABLES),
        out_specs=vmem,
        scratch_shapes=[pltpu.VMEM(single[name].shape, single[name].dtype) for name in TABLES] + [
            flat, flat, flat, flat,
            pltpu.VMEM((32, 16, 128), F32),
            pltpu.VMEM((4096, 32), F32),
            pltpu.VMEM((16, 128, 256), BF16),
            pltpu.VMEM((2, SPECTRAL, WINDOW), BF16),
            pltpu.VMEM((2, WINDOW, SPECTRAL), BF16),
            pltpu.VMEM((2, OWN, OWN), BF16),
            pltpu.VMEM((SPECTRAL, 128), F32),
            grid, grid, grid, grid,
            pltpu.VMEM((4, 2, 48, 128), F32),
            pltpu.VMEM((4, 2, COLS, 128), F32),
            pltpu.VMEM((4, 2, 8, 128), F32),
            pltpu.VMEM((4, 2, 48, 128), F32),
            pltpu.VMEM((4, 2, COLS, 128), F32),
            pltpu.VMEM((4, 2, 8, 128), F32),
            pltpu.SemaphoreType.DMA((len(TABLES),)),
            pltpu.SemaphoreType.DMA((4, 32)),
            pltpu.SemaphoreType.DMA((4, 32)),
            pltpu.SemaphoreType.DMA((4, 5)),
            pltpu.SemaphoreType.DMA((4, 5)),
        ],
        compiler_params=pltpu.CompilerParams(collective_id=1, has_side_effects=True),
        name="step",
    )(stream_speed.reshape(1152, 64), normal_speed.reshape(1152, 64), tables["lift"],
      *[tables[name] for name in TABLES])
    placed = pl.pallas_call(
        place_kernel,
        out_shape=jax.ShapeDtypeStruct((1152, 128), F32),
        in_specs=[vmem],
        out_specs=vmem,
        name="place",
    )(solved)
    return placed.reshape(12, 12, 4, 2, 128)


def solution(mesh):
    return jax.shard_map(
        on_device,
        mesh=mesh,
        in_specs=(P(None, None, "ex", "ey", "mode"), P(None, None, "ex", "ey", "mode")),
        out_specs=P(None, None, "ex", "ey", "mode"),
        check_vma=False,
    )
```

```python
import functools
import math

import jax
import jax.numpy as jnp
import numpy as np
from jax import lax
from jax.experimental import pallas as pl
from jax.experimental.pallas import tpu as pltpu
from jax.sharding import PartitionSpec as P

P_SIZE = 11
NODES = P_SIZE + 1
FINE = 18
FINE_PAD = 336
ELEMS = 4
ROWS_DEV = 2
ROWS_TOTAL = 4
PLANES = 2048
RANKS = 32
LINE = 24
COLS = 48
GRID = COLS * LINE
FLAT = 1024
EXT_POINTS = NODES + 2
OWN = NODES * LINE

MESH = pl.DeviceIdType.MESH
F32 = jnp.float32
BF16 = jnp.bfloat16

element_width = 2.0
shift_base = 10.0
span_rate = 0.0125


def legendre_pair(degree, points):
    before = points * 0.0 + 1.0
    current = points.copy()
    for step in range(1, degree):
        upcoming = ((2 * step + 1) * points * current - step * before) / (step + 1)
        before = current
        current = upcoming
    return (current, before)


def legendre_slope(degree, points):
    current, before = legendre_pair(degree, points)
    return (current, degree * (points * current - before) / (points * points - 1.0))


def lobatto_points(order):
    guesses = -np.cos(np.pi * np.arange(1, order) / order)
    for step in range(60):
        current, slope = legendre_slope(order, guesses)
        second = (2.0 * guesses * slope - order * (order + 1) * current) / (1.0 - guesses * guesses)
        guesses = guesses - slope / second
    return guesses


def gauss_rule(count):
    guesses = -np.cos(np.pi * (np.arange(count) + 0.75) / (count + 0.5))
    for step in range(60):
        current, slope = legendre_slope(count, guesses)
        guesses = guesses - current / slope
    current, slope = legendre_slope(count, guesses)
    return (guesses, 2.0 / ((1.0 - guesses * guesses) * slope * slope))


def jacobi_eigen(matrix):
    size_n = matrix.shape[0]
    work = matrix.copy()
    vectors = np.eye(size_n)
    for sweep_number in range(20):
        for first in range(size_n):
            for second in range(first + 1, size_n):
                coupling = work[first, second]
                if abs(coupling) > 1e-300:
                    theta = (work[second, second] - work[first, first]) / (2.0 * coupling)
                    direction = 1.0 if theta >= 0.0 else -1.0
                    tangent = direction / (abs(theta) + np.sqrt(theta * theta + 1.0))
                    cosine = 1.0 / np.sqrt(tangent * tangent + 1.0)
                    sine = tangent * cosine
                    rotation = np.eye(size_n)
                    rotation[first, first] = cosine
                    rotation[second, second] = cosine
                    rotation[first, second] = sine
                    rotation[second, first] = -sine
                    work = rotation.T @ work @ rotation
                    vectors = vectors @ rotation
    diagonal_index = np.arange(size_n)
    return (work[diagonal_index, diagonal_index], vectors)


def extended_basis(stiffness, weights, left_width, centre_width, right_width):
    node_count = weights.shape[0]
    full_count = 3 * node_count - 2
    stiff_full = np.zeros((full_count, full_count))
    mass_full = np.zeros(full_count)
    for position, span_width in enumerate((left_width, centre_width, right_width)):
        if span_width > 0.0:
            first_node = position * (node_count - 1)
            stiff_full[
                first_node : first_node + node_count, first_node : first_node + node_count
            ] += stiffness * (2.0 / span_width)
            mass_full[first_node : first_node + node_count] += weights * (span_width / 2.0)
    low_index = node_count - 2
    high_index = low_index + node_count + 2
    stiff_ext = stiff_full[low_index:high_index, low_index:high_index].copy()
    mass_ext = mass_full[low_index:high_index].copy()
    frozen_list = []
    if left_width <= 0.0:
        frozen_list += [0, 1]
    if right_width <= 0.0:
        frozen_list += [node_count, node_count + 1]
    for frozen_index in frozen_list:
        stiff_ext[frozen_index, :] = 0.0
        stiff_ext[:, frozen_index] = 0.0
        stiff_ext[frozen_index, frozen_index] = 1.0
        mass_ext[frozen_index] = 1.0
    inverse_root = 1.0 / np.sqrt(mass_ext)
    lambdas, vectors = jacobi_eigen(inverse_root[:, None] * stiff_ext * inverse_root[None, :])
    return (inverse_root[:, None] * vectors, lambdas)


def spectral_tables(order, rows_total):
    inner_points = lobatto_points(order)
    points = np.concatenate([[-1.0], inner_points, [1.0]])
    values, unused_before = legendre_pair(order, points)
    weights = 2.0 / (order * (order + 1) * values**2)
    identity = np.eye(order + 1)
    point_gaps = points[:, None] - points[None, :] + identity
    derivative = values[:, None] / (values[None, :] * point_gaps) * (1.0 - identity)
    derivative[0, 0] = -order * (order + 1) / 4.0
    derivative[order, order] = order * (order + 1) / 4.0
    stiffness = derivative.T @ (weights[:, None] * derivative)
    gauss_points, gauss_weights = gauss_rule(3 * (order + 1) // 2)
    offsets = gauss_points[:, None, None] - points[None, None, :]
    numerators = np.prod(np.where(identity[None, :, :] > 0.5, 1.0, offsets), axis=2)
    denominators = np.prod(np.where(identity > 0.5, 1.0, points[:, None] - points[None, :]), axis=1)
    interp = numerators / denominators[None, :]
    heights = 0.6 + 1.4 * np.sin(np.pi * (np.arange(rows_total) + 0.5) / rows_total)
    basis_x, lambdas_x = extended_basis(
        stiffness, weights, element_width, element_width, element_width
    )
    basis_rows = []
    lambda_rows = []
    for row_number in range(rows_total):
        below = heights[row_number - 1] if row_number > 0 else 0.0
        above = heights[row_number + 1] if row_number < rows_total - 1 else 0.0
        basis_one, lambda_one = extended_basis(
            stiffness, weights, below, heights[row_number], above
        )
        basis_rows.append(basis_one)
        lambda_rows.append(lambda_one)
    return (
        derivative,
        interp,
        gauss_weights,
        weights,
        stiffness,
        basis_x,
        lambdas_x,
        np.stack(basis_rows),
        np.stack(lambda_rows),
        heights,
    )


def bf16_pair(table):
    high = np.asarray(table, np.float32).astype(BF16)
    low = (np.asarray(table, np.float64) - high.astype(np.float64)).astype(np.float32)
    return high, low.astype(BF16)


def split(value):
    high = value.astype(BF16)
    return high, (value - high.astype(F32)).astype(BF16)


def dot(left, right):
    return jnp.dot(left, right, preferred_element_type=F32)


def dot_rows(left, right):
    return lax.dot_general(left, right, (((1,), (1,)), ((), ())), preferred_element_type=F32)


@functools.cache
def all_tables():
    (derivative, interp, gauss_weights, weights, stiffness, basis_x, lambdas_x, basis_y,
     lambdas_y, heights) = spectral_tables(P_SIZE, ROWS_TOTAL)
    nodes = NODES * NODES
    fine = FINE * FINE
    lift = np.zeros((3, FINE_PAD, nodes))
    lift[0, :fine] = np.kron(interp, interp)
    lift[1, :fine] = np.kron(interp @ derivative * (2.0 / element_width), interp)
    lift[2, :fine] = np.kron(interp, interp @ derivative)
    lift = lift.reshape(3 * FINE_PAD, nodes)
    lift_high, lift_low = bf16_pair(lift)
    lift_cat = np.concatenate([lift_high, lift_high, lift_low], 1)
    back = np.zeros((ROWS_DEV, NODES, 16, FINE_PAD))
    quad = np.kron(gauss_weights, gauss_weights)
    back_one = -(np.kron(interp.T, interp.T) * quad[None, :]).reshape(NODES, NODES, fine)
    for f in range(ROWS_DEV):
        back[f, :, 3 * f : 3 * f + NODES, :fine] = back_one
    back_high, back_low = bf16_pair(back.reshape(ROWS_DEV, NODES * 16, FINE_PAD))
    back_cat = np.concatenate([back_high, back_high, back_low], 2)
    plane = np.arange(64)[None, :]
    angle = 2.0 * np.pi * ((np.arange(32)[:, None] * plane) % 64) / 64.0
    wave = np.tile(np.stack([np.cos(angle), np.sin(angle)]), (1, 1, 2))
    twist = np.zeros((16, 4, 2, 2, 64))
    for rp in range(16):
        for half in range(2):
            r = rp if half == 0 else (32 - rp if rp else 16)
            turn = 2.0 * np.pi * r * np.arange(64) / PLANES
            cosine = np.stack([np.cos(turn), -np.sin(turn)]) / PLANES
            sine = np.stack([np.sin(turn), np.cos(turn)]) / PLANES
            if rp == 0:
                twist[rp, 2 * half, :, half] = cosine
                twist[rp, 2 * half + 1, :, half] = -sine
            else:
                sign = 1.0 if half == 0 else -1.0
                twist[rp, 2 * half, :, 0] = cosine
                twist[rp, 2 * half, :, 1] = sign * sine
                twist[rp, 2 * half + 1, :, 0] = -sine
                twist[rp, 2 * half + 1, :, 1] = sign * cosine
    twist = twist.reshape(16, 8, 128)
    line_basis = np.zeros((2, ROWS_DEV, 16, 16))
    line_lambda = np.ones((2, ROWS_DEV, 16))
    line_mass = np.zeros((2, LINE))
    row_mass = np.zeros((2, ROWS_DEV, 16))
    row_stiff = np.zeros((2, ROWS_DEV, 16, 16))
    top = P_SIZE * ROWS_TOTAL
    for ey in range(2):
        for f in range(ROWS_DEV):
            low = 21 * ey + 8 * f
            row = ROWS_DEV * ey + f
            line_lambda[ey, f, :EXT_POINTS] = lambdas_y[row]
            for b in range(EXT_POINTS):
                g = P_SIZE * row + b - 1
                if 0 < g < top:
                    line_basis[ey, f, g - low, :EXT_POINTS] = basis_y[row, b]
            for b in range(NODES):
                g = P_SIZE * row + b
                if 0 < g < top:
                    line_mass[ey, g - 21 * ey] += heights[row] / 2.0 * weights[b]
                    row_mass[ey, f, g - low] = heights[row] / 2.0 * weights[b]
                    for c in range(NODES):
                        h = P_SIZE * row + c
                        if 0 < h < top:
                            row_stiff[ey, f, g - low, h - low] = 2.0 / heights[row] * stiffness[b, c]
    ones_line = np.ones((1, 16))
    in_x = np.kron(basis_x.T, ones_line)
    in_y = np.tile(np.transpose(line_basis, (0, 1, 3, 2)), (1, 1, 1, EXT_POINTS))
    out_x = np.kron(basis_x, ones_line)
    out_y = np.tile(line_basis, (1, 1, 1, EXT_POINTS))
    own_kx = np.kron(stiffness * (2.0 / element_width), ones_line)
    own_my = np.tile(row_mass[..., None] * np.eye(16), (1, 1, 1, NODES))
    own_wx = np.kron(np.diag(weights) * (element_width / 2.0), ones_line)
    own_ky = np.tile(row_stiff, (1, 1, 1, NODES))
    wide = np.ones((1, 1, 128))
    single = dict(lift=lift_cat, back=back_cat)
    single.update({name: np.asarray(table, np.float32) for name, table in dict(
        wave=wave, twist=twist,
        in_x=in_x, in_y=in_y, out_x=out_x, out_y=out_y,
        own_kx=own_kx, own_my=own_my, own_wx=own_wx, own_ky=own_ky,
        mass=line_mass[:, :, None] * wide, lam=line_lambda[..., None] * wide[None]).items()})
    return single, np.asarray(lambdas_x), np.asarray(weights), np.asarray(heights)


def real_transform(values):
    count = len(values)
    if count == 1:
        return [(values[0], None)]
    if count == 2:
        return [(values[0] + values[1], None), (values[0] - values[1], None)]
    even, odd = real_transform(values[0::2]), real_transform(values[1::2])
    quarter, half = count // 4, count // 2
    result = []
    for r in range(half + 1):
        s = r % half

        def pick(part):
            if s <= quarter:
                return part[s], 1.0
            return part[half - s], -1.0

        (er, ei), es = pick(even)
        (dr, di), ds = pick(odd)
        c, n = math.cos(2 * math.pi * r / count), -math.sin(2 * math.pi * r / count)
        if r == 0:
            result.append((er + dr, None))
        elif r == half:
            result.append((er - dr, None))
        elif 4 * r == count:
            result.append((er, -dr))
        else:
            c, n = np.float32(c), np.float32(n)
            if di is None:
                tr, ti = dr * c, dr * n
            else:
                tr = dr * c - di * (n * np.float32(ds))
                ti = dr * n + di * (c * np.float32(ds))
            result.append((er + tr, ti if ei is None else (ti + ei if es > 0 else ti - ei)))
    return result


def flat_row(x):
    return 22 * x if x < 22 else FLAT // 2 + 22 * (x - 22)


RESIDUAL = ((1, 44, 45, 0), (21, 22), (1, 0))
CORRECTION = ((0, 45, 44, 1), (22, 21), (0, 1))
TABLES = ("stream", "normal", "lift", "back", "wave", "twist", "in_x", "in_y", "out_x", "out_y", "own_kx", "own_my", "own_wx",
          "own_ky", "mass", "lam")


def step_kernel(lambdas_x, weights, heights, *refs):
    count = len(TABLES)
    sources, out_ref, refs = refs[:count], refs[count], refs[count + 1 :]
    held, refs = dict(zip(TABLES, refs[:count], strict=True)), refs[count:]
    (weak_out, weak_in, modal_out, modal_in, mid_ref, turn_ref, fourier, inward, outward, local, inverse,
     raw, field, fix, total, side, line, corner, side_in, line_in, corner_in,
     table_sem, share_send, share_recv, send_sem, recv_sem) = refs
    me = lax.axis_index("mode")
    ey = lax.axis_index("ey")
    ex = lax.axis_index("ex")
    low_side = ey == 0
    my_z, my_y, my_c = me // 8, lax.rem(me // 2, 4), lax.rem(me, 2)

    def rank(dz, group):
        dy, dc = group // 2, lax.rem(group, 2)
        return 8 * lax.rem(my_z + dz, 4) + 2 * lax.rem(my_y + dy, 4) + lax.rem(my_c + dc, 2)

    def each_rank(act):
        def apart(i, carry):
            for dz in (2, 1, 3):
                act(dz, lax.rem(i + 4, 8))
            return carry

        def beside(i, carry):
            act(0, i)
            return carry

        lax.fori_loop(0, 8, apart, 0)
        lax.fori_loop(4, 8, beside, 0)
        lax.fori_loop(1, 4, beside, 0)

    loads = [pltpu.make_async_copy(source, held[name], table_sem.at[at])
             for at, (name, source) in enumerate(zip(TABLES, sources, strict=True))]
    for load in loads[:3]:
        load.start()
    u_ref, v_ref, lift_ref = held["stream"], held["normal"], held["lift"]

    left, right, other = lax.rem(ex + 3, 4), lax.rem(ex + 1, 4), 1 - ey
    peers = ({"ex": left, "ey": other}, {"ex": right, "ey": other}, {"ey": other}, {"ex": left}, {"ex": right})
    barrier = pltpu.get_barrier_semaphore()
    each_rank(lambda dz, group: pl.semaphore_signal(
        barrier, inc=1, device_id={"mode": rank(dz, group)}, device_id_type=MESH))
    for peer in peers:
        pl.semaphore_signal(barrier, inc=1, device_id=peer, device_id_type=MESH)
    for load in loads[3:]:
        load.start()
    for load in loads[:3]:
        load.wait()

    def advect(half):
        first = lax.broadcasted_iota(jnp.int32, (FINE_PAD, 128), 1) < 64
        columns = []
        for f in range(ROWS_DEV):
            for e in (2 * half, 2 * half + 1):
                rows = pl.ds(ROWS_DEV * e + f, NODES * NODES, stride=ROWS_DEV * ELEMS)
                columns.append(jnp.concatenate([u_ref[rows, :], v_ref[rows, :]], 1))
        high, low = split(jnp.concatenate(columns, 1))
        fine = dot(lift_ref[...], jnp.concatenate([high, low, high], 0))
        weak = []
        for f in range(ROWS_DEV):
            half_height = jnp.where(
                low_side, np.float32(heights[f] / 2.0), np.float32(heights[ROWS_DEV + f] / 2.0))
            parts = []
            for e in range(2):
                start = 256 * f + 128 * e
                block = slice(start, start + 128)
                speed = fine[:FINE_PAD, block]
                turned = pltpu.roll(speed, 64, 1)
                along = jnp.where(first, speed, turned) * half_height
                across = jnp.where(first, turned, speed)
                parts.append(
                    along * fine[FINE_PAD : 2 * FINE_PAD, block] + across * fine[2 * FINE_PAD :, block])
            high, low = split(jnp.concatenate(parts, 1))
            if half == 0 and f == 0:
                loads[3].wait()
            weak.append(dot(held["back"][f], jnp.concatenate([high, low, high], 0)))
        lines = []
        for a in range(NODES):
            low_row, high_row = slice(16 * a, 16 * a + 8), slice(16 * a + 8, 16 * a + 16)
            lines += [weak[0][low_row], weak[0][high_row] + weak[1][low_row], weak[1][high_row]]
        weak = jnp.concatenate(lines, 0)
        return jnp.where(low_side, pltpu.roll(weak, OWN - 1, 0), weak)

    def store_weak(half, weak, carried):
        for e in range(2):
            for a in range(NODES):
                x = P_SIZE * (2 * half + e) + a
                if a == P_SIZE and x < 44:
                    continue
                value = weak[LINE * a : LINE * a + 22, 128 * e : 128 * e + 128]
                if a == 0 and e == 1:
                    value += weak[LINE * P_SIZE : LINE * P_SIZE + 22, :128]
                if a == 0 and e == 0 and half == 1:
                    value += carried
                weak_out[flat_row(x) : flat_row(x) + 22, :] = value
        spare = (484, 512) if half == 0 else (1018, 1024)
        weak_out[spare[0] : spare[1], :] = jnp.zeros((spare[1] - spare[0], 128), F32)
        return weak[LINE * P_SIZE : LINE * P_SIZE + 22, 128:]

    def send(stage, half):
        source, target = ((weak_out, weak_in), (modal_out, modal_in))[stage]
        base, number = FLAT // 2 * half, 2 * stage + half
        mine = pl.ds(pl.multiple_of(base + 16 * me, 16), 16)

        def start(dz, group):
            peer = rank(dz, group)
            pltpu.make_async_remote_copy(
                src_ref=source.at[pl.ds(pl.multiple_of(base + 16 * peer, 16), 16)],
                dst_ref=target.at[mine],
                send_sem=share_send.at[number],
                recv_sem=share_recv.at[number],
                device_id={"mode": peer},
                device_id_type=MESH,
            ).start()

        each_rank(start)
        target[mine, :] = source[mine, :]

    def bytes_of(stage, half):
        source, target = ((weak_out, weak_in), (modal_out, modal_in))[stage]
        rows, number = pl.ds(0, 16 * (RANKS - 1)), 2 * stage + half
        return pltpu.make_async_remote_copy(
            src_ref=source.at[rows], dst_ref=target.at[rows], send_sem=share_send.at[number],
            recv_sem=share_recv.at[number], device_id={"mode": rank(2, 0)}, device_id_type=MESH)

    def transform(half):
        base = FLAT // 2 * half
        for block in range(2):
            rows = slice(8 * block, 8 * block + 8)
            starts = [base + 16 * d + 8 * block for d in range(RANKS)]
            found = real_transform([weak_in[s : s + 8, :] for s in starts])
            for r in range(1, 16):
                mid_ref[2 * r, rows, :], mid_ref[2 * r + 1, rows, :] = found[r]
            mid_ref[0, rows, :] = found[0][0]
            mid_ref[1, rows, :] = found[16][0]
        first = lax.broadcasted_iota(jnp.int32, (16, 128), 1) < 64
        for rp in range(16):
            real, imag = mid_ref[2 * rp], mid_ref[2 * rp + 1]
            both = jnp.concatenate(
                [jnp.where(first, real, pltpu.roll(imag, 64, 1)),
                 jnp.where(first, pltpu.roll(real, 64, 1), imag)], 0)
            high, low = split(both)
            table = fourier[rp]
            found = dot_rows(table, jnp.concatenate([high, high], 1)) + dot_rows(table[:, :128], low)
            for at in range(2):
                r = rp if at == 0 else (32 - rp if rp else 16)
                for c in range(2):
                    start = 32 * (2 * at + c)
                    for k in range(2):
                        turn_ref[pl.ds(4 * r + 2 * c + k, 32, stride=128), :] = found[start : start + 32, :]
        even = lax.broadcasted_iota(jnp.int32, (16, 128), 1) % 2 == 0
        for q in range(RANKS):
            turned = turn_ref[128 * q : 128 * q + 128, :].T
            modal_out[base + 16 * q : base + 16 * q + 16, :] = jnp.where(even, turned[:16], turned[16:])

    carried = store_weak(0, advect(0), None)
    store_weak(1, advect(1), carried)
    pl.semaphore_wait(barrier, RANKS - 1 + 5)
    send(0, 0)
    send(0, 1)

    for load in loads[4:]:
        load.wait()
    for rp in range(16):
        for at in range(4):
            pair = held["twist"][rp, 2 * at : 2 * at + 2, :]
            high, low = split(held["wave"][0] * pair[:1] + held["wave"][1] * pair[1:])
            fourier[rp, 32 * at : 32 * at + 32, :128] = high
            fourier[rp, 32 * at : 32 * at + 32, 128:] = low
    lane = lax.broadcasted_iota(jnp.int32, (1, 128), 1)
    mode = (me * 32 + lane // 4).astype(F32)
    shift = shift_base + (np.float32(span_rate) * mode) ** 2
    for f in range(ROWS_DEV):
        for i in range(EXT_POINTS):
            rows = slice(16 * i, 16 * i + 16)
            high, low = split(held["in_x"][i : i + 1, :] * held["in_y"][ey, f])
            inward[f, 0, rows, :], inward[f, 1, rows, :] = high, low
            high, low = split(held["out_x"][i : i + 1, :] * held["out_y"][ey, f])
            outward[f, 0, rows, :], outward[f, 1, rows, :] = high, low
            inverse[f, rows, :] = 1.0 / (held["lam"][ey, f] + (shift + np.float32(lambdas_x[i])))
        for a in range(NODES):
            rows = slice(16 * a, 16 * a + 16)
            high, low = split(
                held["own_kx"][a : a + 1, :] * held["own_my"][ey, f]
                + held["own_wx"][a : a + 1, :] * held["own_ky"][ey, f])
            local[f, 0, rows, :], local[f, 1, rows, :] = high, low
    mass_shift = [held["mass"][ey, 8 * g : 8 * g + 8, :] * shift for g in range(3)]
    raw[...] = jnp.zeros((GRID, 128), F32)

    for half in range(2):
        bytes_of(0, half).wait_recv()
        transform(half)
        send(1, half)
    for half in range(2):
        bytes_of(1, half).wait_recv()
        for x in range(22 * half, 22 + 23 * half):
            raw[LINE * (x + 1) + 1 : LINE * (x + 1) + 23, :] = modal_in[flat_row(x) : flat_row(x) + 22, :]

    def all_of(number, rows, at):
        return pltpu.make_async_remote_copy(
            src_ref=raw.at[pl.ds(0, rows)], dst_ref=raw.at[pl.ds(0, rows)], send_sem=send_sem.at[number],
            recv_sem=recv_sem.at[number, at], device_id=peers[2], device_id_type=MESH)

    def exchange(number, grid, kind):
        (to_left, to_right, from_right, from_left), lower, upper = kind
        zero = jnp.zeros((4, 128), F32)
        pieces = []
        for step in range(2):
            rows = jnp.where(
                low_side,
                grid[pl.ds(lower[0] + step, COLS, stride=LINE), :],
                grid[pl.ds(upper[0] + step, COLS, stride=LINE), :])
            line[number, step] = rows
            pieces.append(rows)
        for at, column in enumerate((to_left, to_right)):
            corner[number, at] = jnp.concatenate([p[column : column + 2] for p in pieces] + [zero], 0)
        side[number, 0] = grid[LINE * to_left : LINE * to_left + 48, :]
        side[number, 1] = grid[LINE * to_right : LINE * to_right + 48, :]
        sends = (
            (corner.at[number, 0], corner_in.at[number, 0]),
            (corner.at[number, 1], corner_in.at[number, 1]),
            (line.at[number], line_in.at[number]),
            (side.at[number, 0], side_in.at[number, 0]),
            (side.at[number, 1], side_in.at[number, 1]))
        for at, ((source, target), peer) in enumerate(zip(sends, peers, strict=True)):
            pltpu.make_async_remote_copy(
                src_ref=source, dst_ref=target, send_sem=send_sem.at[number],
                recv_sem=recv_sem.at[number, at // 3], device_id=peer, device_id_type=MESH).start()
        all_of(number, 96, 1).wait_recv()
        grid[LINE * from_right : LINE * from_right + 48, :] += side_in[number, 0]
        grid[LINE * from_left : LINE * from_left + 48, :] += side_in[number, 1]
        all_of(number, 112, 0).wait_recv()
        zeros = jnp.zeros((COLS, 128), F32)
        for step in range(2):
            rows = [line_in[number, step]]
            for at, column in enumerate((from_right, from_left)):
                piece = corner_in[number, at, 2 * step : 2 * step + 2, :]
                before = [jnp.zeros((column, 128), F32)] if column else []
                rows.append(jnp.concatenate(
                    before + [piece, jnp.zeros((COLS - 2 - column, 128), F32)], 0))
            added = rows[0] + rows[1] + rows[2]
            where_low = pl.ds(lower[1] + step, COLS, stride=LINE)
            where_up = pl.ds(upper[1] + step, COLS, stride=LINE)
            grid[where_low, :] += jnp.where(low_side, added, zeros)
            grid[where_up, :] += jnp.where(low_side, zeros, added)

    def rows_of(source, f, first, count):
        return jnp.concatenate(
            [jnp.concatenate(
                [source[264 * e + LINE * (first + a) + 8 * f : 264 * e + LINE * (first + a) + 8 * f + 16, :]
                 for a in range(count)], 0) for e in range(ELEMS)], 1)

    def apply(matrix, value):
        high, low = split(value)
        return dot(matrix[0], high) + dot(matrix[0], low) + dot(matrix[1], high)

    def gathered(parts, x, g, first, count):
        found = None
        for e in range(ELEMS):
            a = x - P_SIZE * e - first
            if not 0 <= a < count:
                continue
            for f in range(ROWS_DEV):
                if 0 <= g - f < 2:
                    row = 16 * a + 8 * (g - f)
                    term = parts[f][row : row + 8, 128 * e : 128 * e + 128]
                    found = term if found is None else found + term
        return found

    def solve(source, target):
        parts = []
        for f in range(ROWS_DEV):
            modal = apply(inward.at[f], rows_of(source, f, 0, EXT_POINTS))
            parts.append(apply(outward.at[f], modal * jnp.concatenate([inverse[f]] * ELEMS, 1)))
        for x in range(COLS):
            for g in range(3):
                found = gathered(parts, x, g, 0, EXT_POINTS)
                row = LINE * x + 8 * g
                target[row : row + 8, :] = jnp.zeros((8, 128), F32) if found is None else found

    field[...] = raw[...]
    exchange(0, field, RESIDUAL)
    solve(field, total)
    exchange(1, total, CORRECTION)
    parts = [apply(local.at[f], rows_of(total, f, 1, NODES)) for f in range(ROWS_DEV)]
    for x in range(COLS):
        for g in range(3):
            row = LINE * x + 8 * g
            found = gathered(parts, x, g, 1, NODES)
            if found is None:
                field[row : row + 8, :] = jnp.zeros((8, 128), F32)
                continue
            mass_x = sum(weights[x - P_SIZE * e - 1] * element_width / 2.0
                         for e in range(ELEMS) if 0 <= x - P_SIZE * e - 1 < NODES)
            field[row : row + 8, :] = (
                raw[row : row + 8, :] - found - (mass_shift[g] * np.float32(mass_x)) * total[row : row + 8, :])
    exchange(2, field, RESIDUAL)
    solve(field, fix)
    exchange(3, fix, CORRECTION)
    out_ref[...] = total[...] + fix[...]
    for number in range(4):
        all_of(number, 208, 0).wait_send()
    for stage in range(2):
        for half in range(2):
            bytes_of(stage, half).wait_send()


def place_kernel(grid_ref, out_ref):
    low_side = lax.axis_index("ey") == 0
    for e in range(ELEMS):
        for f in range(ROWS_DEV):
            for a in range(NODES):
                start = LINE * (P_SIZE * e + 1 + a) + P_SIZE * f
                out_ref[pl.ds(96 * a + 2 * e + f, NODES, stride=8), :] = jnp.where(
                    low_side, grid_ref[start : start + NODES, :], grid_ref[start + 1 : start + 1 + NODES, :])


def on_device(stream_speed, normal_speed):
    single, lambdas_x, weights, heights = all_tables()
    vmem = pl.BlockSpec(memory_space=pltpu.VMEM)
    anywhere = pl.BlockSpec(memory_space=pl.ANY)
    tables = {name: jnp.asarray(table) for name, table in single.items()}
    tables["stream"] = stream_speed.reshape(1152, 64)
    tables["normal"] = normal_speed.reshape(1152, 64)
    given = [tables[name] for name in TABLES]
    grid = pltpu.VMEM((GRID, 128), F32)
    flat = pltpu.VMEM((FLAT, 128), F32)
    solved = pl.pallas_call(
        functools.partial(step_kernel, lambdas_x, weights, heights),
        out_shape=jax.ShapeDtypeStruct((GRID, 128), F32),
        in_specs=[anywhere] * len(TABLES),
        out_specs=vmem,
        scratch_shapes=[pltpu.VMEM(table.shape, table.dtype) for table in given] + [
            flat, flat, flat, flat,
            pltpu.VMEM((32, 16, 128), F32),
            pltpu.VMEM((4096, 32), F32),
            pltpu.VMEM((16, 128, 256), BF16),
            pltpu.VMEM((2, 2, EXT_POINTS * 16, EXT_POINTS * 16), BF16),
            pltpu.VMEM((2, 2, EXT_POINTS * 16, EXT_POINTS * 16), BF16),
            pltpu.VMEM((2, 2, NODES * 16, NODES * 16), BF16),
            pltpu.VMEM((2, EXT_POINTS * 16, 128), F32),
            grid, grid, grid, grid,
            pltpu.VMEM((4, 2, 48, 128), F32),
            pltpu.VMEM((4, 2, COLS, 128), F32),
            pltpu.VMEM((4, 2, 8, 128), F32),
            pltpu.VMEM((4, 2, 48, 128), F32),
            pltpu.VMEM((4, 2, COLS, 128), F32),
            pltpu.VMEM((4, 2, 8, 128), F32),
            pltpu.SemaphoreType.DMA((len(TABLES),)),
            pltpu.SemaphoreType.DMA((4,)),
            pltpu.SemaphoreType.DMA((4,)),
            pltpu.SemaphoreType.DMA((4,)),
            pltpu.SemaphoreType.DMA((4, 2)),
        ],
        compiler_params=pltpu.CompilerParams(collective_id=1, has_side_effects=True),
        name="step",
    )(*given)
    placed = pl.pallas_call(
        place_kernel,
        out_shape=jax.ShapeDtypeStruct((1152, 128), F32),
        in_specs=[vmem],
        out_specs=vmem,
        name="place",
    )(solved)
    return placed.reshape(12, 12, 4, 2, 128)


def solution(mesh):
    return jax.shard_map(
        on_device,
        mesh=mesh,
        in_specs=(P(None, None, "ex", "ey", "mode"), P(None, None, "ex", "ey", "mode")),
        out_specs=P(None, None, "ex", "ey", "mode"),
        check_vma=False,
    )
```

```python
import functools
import math

import jax
import jax.numpy as jnp
import numpy as np
from jax import lax
from jax.experimental import pallas as pl
from jax.experimental.pallas import tpu as pltpu
from jax.sharding import PartitionSpec as P

P_SIZE = 11
NODES = P_SIZE + 1
FINE = 18
FINE_PAD = 336
ELEMS = 4
ROWS_DEV = 2
ROWS_TOTAL = 4
PLANES = 2048
RANKS = 32
LINE = 24
COLS = 48
GRID = COLS * LINE
FLAT = 1024
EXT_POINTS = NODES + 2
OWN = NODES * LINE

MESH = pl.DeviceIdType.MESH
F32 = jnp.float32
BF16 = jnp.bfloat16

element_width = 2.0
shift_base = 10.0
span_rate = 0.0125


def legendre_pair(degree, points):
    before = points * 0.0 + 1.0
    current = points.copy()
    for step in range(1, degree):
        upcoming = ((2 * step + 1) * points * current - step * before) / (step + 1)
        before = current
        current = upcoming
    return (current, before)


def legendre_slope(degree, points):
    current, before = legendre_pair(degree, points)
    return (current, degree * (points * current - before) / (points * points - 1.0))


def lobatto_points(order):
    guesses = -np.cos(np.pi * np.arange(1, order) / order)
    for step in range(60):
        current, slope = legendre_slope(order, guesses)
        second = (2.0 * guesses * slope - order * (order + 1) * current) / (1.0 - guesses * guesses)
        guesses = guesses - slope / second
    return guesses


def gauss_rule(count):
    guesses = -np.cos(np.pi * (np.arange(count) + 0.75) / (count + 0.5))
    for step in range(60):
        current, slope = legendre_slope(count, guesses)
        guesses = guesses - current / slope
    current, slope = legendre_slope(count, guesses)
    return (guesses, 2.0 / ((1.0 - guesses * guesses) * slope * slope))


def jacobi_eigen(matrix):
    size_n = matrix.shape[0]
    work = matrix.copy()
    vectors = np.eye(size_n)
    for sweep_number in range(20):
        for first in range(size_n):
            for second in range(first + 1, size_n):
                coupling = work[first, second]
                if abs(coupling) > 1e-300:
                    theta = (work[second, second] - work[first, first]) / (2.0 * coupling)
                    direction = 1.0 if theta >= 0.0 else -1.0
                    tangent = direction / (abs(theta) + np.sqrt(theta * theta + 1.0))
                    cosine = 1.0 / np.sqrt(tangent * tangent + 1.0)
                    sine = tangent * cosine
                    rotation = np.eye(size_n)
                    rotation[first, first] = cosine
                    rotation[second, second] = cosine
                    rotation[first, second] = sine
                    rotation[second, first] = -sine
                    work = rotation.T @ work @ rotation
                    vectors = vectors @ rotation
    diagonal_index = np.arange(size_n)
    return (work[diagonal_index, diagonal_index], vectors)


def extended_basis(stiffness, weights, left_width, centre_width, right_width):
    node_count = weights.shape[0]
    full_count = 3 * node_count - 2
    stiff_full = np.zeros((full_count, full_count))
    mass_full = np.zeros(full_count)
    for position, span_width in enumerate((left_width, centre_width, right_width)):
        if span_width > 0.0:
            first_node = position * (node_count - 1)
            stiff_full[
                first_node : first_node + node_count, first_node : first_node + node_count
            ] += stiffness * (2.0 / span_width)
            mass_full[first_node : first_node + node_count] += weights * (span_width / 2.0)
    low_index = node_count - 2
    high_index = low_index + node_count + 2
    stiff_ext = stiff_full[low_index:high_index, low_index:high_index].copy()
    mass_ext = mass_full[low_index:high_index].copy()
    frozen_list = []
    if left_width <= 0.0:
        frozen_list += [0, 1]
    if right_width <= 0.0:
        frozen_list += [node_count, node_count + 1]
    for frozen_index in frozen_list:
        stiff_ext[frozen_index, :] = 0.0
        stiff_ext[:, frozen_index] = 0.0
        stiff_ext[frozen_index, frozen_index] = 1.0
        mass_ext[frozen_index] = 1.0
    inverse_root = 1.0 / np.sqrt(mass_ext)
    lambdas, vectors = jacobi_eigen(inverse_root[:, None] * stiff_ext * inverse_root[None, :])
    return (inverse_root[:, None] * vectors, lambdas)


def spectral_tables(order, rows_total):
    inner_points = lobatto_points(order)
    points = np.concatenate([[-1.0], inner_points, [1.0]])
    values, unused_before = legendre_pair(order, points)
    weights = 2.0 / (order * (order + 1) * values**2)
    identity = np.eye(order + 1)
    point_gaps = points[:, None] - points[None, :] + identity
    derivative = values[:, None] / (values[None, :] * point_gaps) * (1.0 - identity)
    derivative[0, 0] = -order * (order + 1) / 4.0
    derivative[order, order] = order * (order + 1) / 4.0
    stiffness = derivative.T @ (weights[:, None] * derivative)
    gauss_points, gauss_weights = gauss_rule(3 * (order + 1) // 2)
    offsets = gauss_points[:, None, None] - points[None, None, :]
    numerators = np.prod(np.where(identity[None, :, :] > 0.5, 1.0, offsets), axis=2)
    denominators = np.prod(np.where(identity > 0.5, 1.0, points[:, None] - points[None, :]), axis=1)
    interp = numerators / denominators[None, :]
    heights = 0.6 + 1.4 * np.sin(np.pi * (np.arange(rows_total) + 0.5) / rows_total)
    basis_x, lambdas_x = extended_basis(
        stiffness, weights, element_width, element_width, element_width
    )
    basis_rows = []
    lambda_rows = []
    for row_number in range(rows_total):
        below = heights[row_number - 1] if row_number > 0 else 0.0
        above = heights[row_number + 1] if row_number < rows_total - 1 else 0.0
        basis_one, lambda_one = extended_basis(
            stiffness, weights, below, heights[row_number], above
        )
        basis_rows.append(basis_one)
        lambda_rows.append(lambda_one)
    return (
        derivative,
        interp,
        gauss_weights,
        weights,
        stiffness,
        basis_x,
        lambdas_x,
        np.stack(basis_rows),
        np.stack(lambda_rows),
        heights,
    )


def bf16_pair(table):
    high = np.asarray(table, np.float32).astype(BF16)
    low = (np.asarray(table, np.float64) - high.astype(np.float64)).astype(np.float32)
    return high, low.astype(BF16)


def split(value):
    high = value.astype(BF16)
    return high, (value - high.astype(F32)).astype(BF16)


def dot(left, right):
    return jnp.dot(left, right, preferred_element_type=F32)


def dot_rows(left, right):
    return lax.dot_general(left, right, (((1,), (1,)), ((), ())), preferred_element_type=F32)


SMALL = (("wave", 64, 128), ("twist", 128, 128), ("in_x", 16, 224), ("in_y", 64, 224), ("out_x", 16, 224),
         ("out_y", 64, 224), ("own_kx", 16, 192), ("own_my", 64, 192), ("own_wx", 16, 192), ("own_ky", 64, 192),
         ("mass", 48, 128), ("lam", 64, 128))
SMALL_AT = {entry[0]: sum(other[1] for other in SMALL[:at]) for at, entry in enumerate(SMALL)}
SMALL_WIDTH = {name: width for name, _, width in SMALL}


@functools.cache
def all_tables():
    (derivative, interp, gauss_weights, weights, stiffness, basis_x, lambdas_x, basis_y,
     lambdas_y, heights) = spectral_tables(P_SIZE, ROWS_TOTAL)
    nodes = NODES * NODES
    fine = FINE * FINE
    lift = np.zeros((3, FINE_PAD, nodes))
    lift[0, :fine] = np.kron(interp, interp)
    lift[1, :fine] = np.kron(interp @ derivative * (2.0 / element_width), interp)
    lift[2, :fine] = np.kron(interp, interp @ derivative)
    lift = lift.reshape(3 * FINE_PAD, nodes)
    lift_high, lift_low = bf16_pair(lift)
    lift_cat = np.concatenate([lift_high, lift_high, lift_low], 1)
    back = np.zeros((ROWS_DEV, NODES, 16, FINE_PAD))
    quad = np.kron(gauss_weights, gauss_weights)
    back_one = -(np.kron(interp.T, interp.T) * quad[None, :]).reshape(NODES, NODES, fine)
    for f in range(ROWS_DEV):
        back[f, :, 3 * f : 3 * f + NODES, :fine] = back_one
    back_high, back_low = bf16_pair(back.reshape(ROWS_DEV, NODES * 16, FINE_PAD))
    back_cat = np.concatenate([back_high, back_high, back_low], 2)
    plane = np.arange(64)[None, :]
    angle = 2.0 * np.pi * ((np.arange(32)[:, None] * plane) % 64) / 64.0
    wave = np.tile(np.stack([np.cos(angle), np.sin(angle)]), (1, 1, 2))
    twist = np.zeros((16, 4, 2, 2, 64))
    for rp in range(16):
        for half in range(2):
            r = rp if half == 0 else (32 - rp if rp else 16)
            turn = 2.0 * np.pi * r * np.arange(64) / PLANES
            cosine = np.stack([np.cos(turn), -np.sin(turn)]) / PLANES
            sine = np.stack([np.sin(turn), np.cos(turn)]) / PLANES
            if rp == 0:
                twist[rp, 2 * half, :, half] = cosine
                twist[rp, 2 * half + 1, :, half] = -sine
            else:
                sign = 1.0 if half == 0 else -1.0
                twist[rp, 2 * half, :, 0] = cosine
                twist[rp, 2 * half, :, 1] = sign * sine
                twist[rp, 2 * half + 1, :, 0] = -sine
                twist[rp, 2 * half + 1, :, 1] = sign * cosine
    twist = twist.reshape(16, 8, 128)
    line_basis = np.zeros((2, ROWS_DEV, 16, 16))
    line_lambda = np.ones((2, ROWS_DEV, 16))
    line_mass = np.zeros((2, LINE))
    row_mass = np.zeros((2, ROWS_DEV, 16))
    row_stiff = np.zeros((2, ROWS_DEV, 16, 16))
    top = P_SIZE * ROWS_TOTAL
    for ey in range(2):
        for f in range(ROWS_DEV):
            low = 21 * ey + 8 * f
            row = ROWS_DEV * ey + f
            line_lambda[ey, f, :EXT_POINTS] = lambdas_y[row]
            for b in range(EXT_POINTS):
                g = P_SIZE * row + b - 1
                if 0 < g < top:
                    line_basis[ey, f, g - low, :EXT_POINTS] = basis_y[row, b]
            for b in range(NODES):
                g = P_SIZE * row + b
                if 0 < g < top:
                    line_mass[ey, g - 21 * ey] += heights[row] / 2.0 * weights[b]
                    row_mass[ey, f, g - low] = heights[row] / 2.0 * weights[b]
                    for c in range(NODES):
                        h = P_SIZE * row + c
                        if 0 < h < top:
                            row_stiff[ey, f, g - low, h - low] = 2.0 / heights[row] * stiffness[b, c]
    ones_line = np.ones((1, 16))
    in_x = np.kron(basis_x.T, ones_line)
    in_y = np.tile(np.transpose(line_basis, (0, 1, 3, 2)), (1, 1, 1, EXT_POINTS))
    out_x = np.kron(basis_x, ones_line)
    out_y = np.tile(line_basis, (1, 1, 1, EXT_POINTS))
    own_kx = np.kron(stiffness * (2.0 / element_width), ones_line)
    own_my = np.tile(row_mass[..., None] * np.eye(16), (1, 1, 1, NODES))
    own_wx = np.kron(np.diag(weights) * (element_width / 2.0), ones_line)
    own_ky = np.tile(row_stiff, (1, 1, 1, NODES))
    wide = np.ones((1, 1, 128))
    named = dict(
        wave=wave, twist=twist, in_x=in_x, in_y=in_y, out_x=out_x, out_y=out_y, own_kx=own_kx, own_my=own_my,
        own_wx=own_wx, own_ky=own_ky, mass=line_mass[:, :, None] * wide, lam=line_lambda[..., None] * wide[None])
    small = np.zeros((sum(rows for _, rows, _ in SMALL), 256), np.float32)
    for name, rows, width in SMALL:
        table = named[name].reshape(-1, width)
        small[SMALL_AT[name] : SMALL_AT[name] + table.shape[0], :width] = table
    single = dict(lift=lift_cat, back=back_cat, small=small)
    return single, np.asarray(lambdas_x), np.asarray(weights), np.asarray(heights)


def real_transform(values):
    count = len(values)
    if count == 1:
        return [(values[0], None)]
    if count == 2:
        return [(values[0] + values[1], None), (values[0] - values[1], None)]
    even, odd = real_transform(values[0::2]), real_transform(values[1::2])
    quarter, half = count // 4, count // 2
    result = []
    for r in range(half + 1):
        s = r % half

        def pick(part):
            if s <= quarter:
                return part[s], 1.0
            return part[half - s], -1.0

        (er, ei), es = pick(even)
        (dr, di), ds = pick(odd)
        c, n = math.cos(2 * math.pi * r / count), -math.sin(2 * math.pi * r / count)
        if r == 0:
            result.append((er + dr, None))
        elif r == half:
            result.append((er - dr, None))
        elif 4 * r == count:
            result.append((er, -dr))
        else:
            c, n = np.float32(c), np.float32(n)
            if di is None:
                tr, ti = dr * c, dr * n
            else:
                tr = dr * c - di * (n * np.float32(ds))
                ti = dr * n + di * (c * np.float32(ds))
            result.append((er + tr, ti if ei is None else (ti + ei if es > 0 else ti - ei)))
    return result


def flat_row(x):
    return 22 * x if x < 22 else FLAT // 2 + 22 * (x - 22)


RESIDUAL = ((1, 44, 45, 0), (21, 22), (1, 0))
CORRECTION = ((0, 45, 44, 1), (22, 21), (0, 1))
TABLES = ("stream", "normal", "lift", "back", "small")


def step_kernel(lambdas_x, weights, heights, *refs):
    count = len(TABLES)
    sources, out_ref, refs = refs[:count], refs[count], refs[count + 1 :]
    held, refs = dict(zip(TABLES, refs[:count], strict=True)), refs[count:]
    (weak_out, weak_in, modal_out, modal_in, mid_ref, turn_ref, fourier, inward, outward, local, inverse,
     raw, field, fix, total, side, line, corner, side_in, line_in, corner_in,
     table_sem, share_send, share_recv, send_sem, recv_sem) = refs
    me = lax.axis_index("mode")
    ey = lax.axis_index("ey")
    ex = lax.axis_index("ex")
    low_side = ey == 0
    my_z, my_y, my_c = me // 8, lax.rem(me // 2, 4), lax.rem(me, 2)

    def rank(dz, group):
        dy, dc = group // 2, lax.rem(group, 2)
        return 8 * lax.rem(my_z + dz, 4) + 2 * lax.rem(my_y + dy, 4) + lax.rem(my_c + dc, 2)

    def each_rank(act):
        def apart(i, carry):
            for dz in (2, 1, 3):
                act(dz, lax.rem(i + 4, 8))
            return carry

        def beside(i, carry):
            act(0, i)
            return carry

        lax.fori_loop(0, 8, apart, 0)
        lax.fori_loop(4, 8, beside, 0)
        lax.fori_loop(1, 4, beside, 0)

    loads = [pltpu.make_async_copy(source, held[name], table_sem.at[at])
             for at, (name, source) in enumerate(zip(TABLES, sources, strict=True))]
    for load in loads[:3]:
        load.start()
    u_ref, v_ref, lift_ref = held["stream"], held["normal"], held["lift"]

    left, right, other = lax.rem(ex + 3, 4), lax.rem(ex + 1, 4), 1 - ey
    peers = ({"ex": left, "ey": other}, {"ex": right, "ey": other}, {"ey": other}, {"ex": left}, {"ex": right})
    barrier = pltpu.get_barrier_semaphore()
    each_rank(lambda dz, group: pl.semaphore_signal(
        barrier, inc=1, device_id={"mode": rank(dz, group)}, device_id_type=MESH))
    for peer in peers:
        pl.semaphore_signal(barrier, inc=1, device_id=peer, device_id_type=MESH)
    for load in loads[3:]:
        load.start()
    for load in loads[:3]:
        load.wait()

    def advect(half):
        first = lax.broadcasted_iota(jnp.int32, (FINE_PAD, 128), 1) < 64
        columns = []
        for f in range(ROWS_DEV):
            for e in (2 * half, 2 * half + 1):
                rows = pl.ds(ROWS_DEV * e + f, NODES * NODES, stride=ROWS_DEV * ELEMS)
                columns.append(jnp.concatenate([u_ref[rows, :], v_ref[rows, :]], 1))
        high, low = split(jnp.concatenate(columns, 1))
        fine = dot(lift_ref[...], jnp.concatenate([high, low, high], 0))
        weak = []
        for f in range(ROWS_DEV):
            half_height = jnp.where(
                low_side, np.float32(heights[f] / 2.0), np.float32(heights[ROWS_DEV + f] / 2.0))
            parts = []
            for e in range(2):
                start = 256 * f + 128 * e
                block = slice(start, start + 128)
                speed = fine[:FINE_PAD, block]
                turned = pltpu.roll(speed, 64, 1)
                along = jnp.where(first, speed, turned) * half_height
                across = jnp.where(first, turned, speed)
                parts.append(
                    along * fine[FINE_PAD : 2 * FINE_PAD, block] + across * fine[2 * FINE_PAD :, block])
            high, low = split(jnp.concatenate(parts, 1))
            if half == 0 and f == 0:
                loads[3].wait()
            weak.append(dot(held["back"][f], jnp.concatenate([high, low, high], 0)))
        lines = []
        for a in range(NODES):
            low_row, high_row = slice(16 * a, 16 * a + 8), slice(16 * a + 8, 16 * a + 16)
            lines += [weak[0][low_row], weak[0][high_row] + weak[1][low_row], weak[1][high_row]]
        weak = jnp.concatenate(lines, 0)
        return jnp.where(low_side, pltpu.roll(weak, OWN - 1, 0), weak)

    def store_weak(half, weak, carried):
        for e in range(2):
            for a in range(NODES):
                x = P_SIZE * (2 * half + e) + a
                if a == P_SIZE and x < 44:
                    continue
                value = weak[LINE * a : LINE * a + 22, 128 * e : 128 * e + 128]
                if a == 0 and e == 1:
                    value += weak[LINE * P_SIZE : LINE * P_SIZE + 22, :128]
                if a == 0 and e == 0 and half == 1:
                    value += carried
                weak_out[flat_row(x) : flat_row(x) + 22, :] = value
        spare = (484, 512) if half == 0 else (1018, 1024)
        weak_out[spare[0] : spare[1], :] = jnp.zeros((spare[1] - spare[0], 128), F32)
        return weak[LINE * P_SIZE : LINE * P_SIZE + 22, 128:]

    def send(stage, half):
        source, target = ((weak_out, weak_in), (modal_out, modal_in))[stage]
        base, number = FLAT // 2 * half, 2 * stage + half
        mine = pl.ds(pl.multiple_of(base + 16 * me, 16), 16)

        def start(dz, group):
            peer = rank(dz, group)
            pltpu.make_async_remote_copy(
                src_ref=source.at[pl.ds(pl.multiple_of(base + 16 * peer, 16), 16)],
                dst_ref=target.at[mine],
                send_sem=share_send.at[number],
                recv_sem=share_recv.at[number],
                device_id={"mode": peer},
                device_id_type=MESH,
            ).start()

        each_rank(start)
        target[mine, :] = source[mine, :]

    def bytes_of(stage, half):
        source, target = ((weak_out, weak_in), (modal_out, modal_in))[stage]
        rows, number = pl.ds(0, 16 * (RANKS - 1)), 2 * stage + half
        return pltpu.make_async_remote_copy(
            src_ref=source.at[rows], dst_ref=target.at[rows], send_sem=share_send.at[number],
            recv_sem=share_recv.at[number], device_id={"mode": rank(2, 0)}, device_id_type=MESH)

    def transform(half):
        base = FLAT // 2 * half
        for block in range(2):
            rows = slice(8 * block, 8 * block + 8)
            starts = [base + 16 * d + 8 * block for d in range(RANKS)]
            found = real_transform([weak_in[s : s + 8, :] for s in starts])
            for r in range(1, 16):
                mid_ref[2 * r, rows, :], mid_ref[2 * r + 1, rows, :] = found[r]
            mid_ref[0, rows, :] = found[0][0]
            mid_ref[1, rows, :] = found[16][0]
        first = lax.broadcasted_iota(jnp.int32, (16, 128), 1) < 64
        for rp in range(16):
            real, imag = mid_ref[2 * rp], mid_ref[2 * rp + 1]
            both = jnp.concatenate(
                [jnp.where(first, real, pltpu.roll(imag, 64, 1)),
                 jnp.where(first, pltpu.roll(real, 64, 1), imag)], 0)
            high, low = split(both)
            table = fourier[rp]
            found = dot_rows(table, jnp.concatenate([high, high], 1)) + dot_rows(table[:, :128], low)
            for at in range(2):
                r = rp if at == 0 else (32 - rp if rp else 16)
                for c in range(2):
                    start = 32 * (2 * at + c)
                    for k in range(2):
                        turn_ref[pl.ds(4 * r + 2 * c + k, 32, stride=128), :] = found[start : start + 32, :]
        even = lax.broadcasted_iota(jnp.int32, (16, 128), 1) % 2 == 0
        for q in range(RANKS):
            turned = turn_ref[128 * q : 128 * q + 128, :].T
            modal_out[base + 16 * q : base + 16 * q + 16, :] = jnp.where(even, turned[:16], turned[16:])

    carried = store_weak(0, advect(0), None)
    pl.semaphore_wait(barrier, RANKS - 1 + 5)
    send(0, 0)
    store_weak(1, advect(1), carried)
    send(0, 1)

    def part(name, start, count):
        return held["small"][pl.ds(SMALL_AT[name] + start, count), : SMALL_WIDTH[name]]

    def row_part(name, f):
        start = pl.multiple_of(SMALL_AT[name] + 16 * (ROWS_DEV * ey + f), 16)
        return held["small"][pl.ds(start, 16), : SMALL_WIDTH[name]]

    for load in loads[4:]:
        load.wait()
    for rp in range(16):
        for at in range(4):
            pair = part("twist", 8 * rp + 2 * at, 2)
            high, low = split(part("wave", 0, 32) * pair[:1] + part("wave", 32, 32) * pair[1:])
            fourier[rp, 32 * at : 32 * at + 32, :128] = high
            fourier[rp, 32 * at : 32 * at + 32, 128:] = low
    lane = lax.broadcasted_iota(jnp.int32, (1, 128), 1)
    mode = (me * 32 + lane // 4).astype(F32)
    shift = shift_base + (np.float32(span_rate) * mode) ** 2
    for f in range(ROWS_DEV):
        for i in range(EXT_POINTS):
            rows = slice(16 * i, 16 * i + 16)
            high, low = split(part("in_x", i, 1) * row_part("in_y", f))
            inward[f, 0, rows, :], inward[f, 1, rows, :] = high, low
            high, low = split(part("out_x", i, 1) * row_part("out_y", f))
            outward[f, 0, rows, :], outward[f, 1, rows, :] = high, low
            inverse[f, rows, :] = 1.0 / (row_part("lam", f) + (shift + np.float32(lambdas_x[i])))
        for a in range(NODES):
            rows = slice(16 * a, 16 * a + 16)
            high, low = split(
                part("own_kx", a, 1) * row_part("own_my", f)
                + part("own_wx", a, 1) * row_part("own_ky", f))
            local[f, 0, rows, :], local[f, 1, rows, :] = high, low
    mass_shift = [held["small"][pl.ds(pl.multiple_of(SMALL_AT["mass"] + LINE * ey + 8 * g, 8), 8), :128] * shift for g in range(3)]
    raw[...] = jnp.zeros((GRID, 128), F32)

    for half in range(2):
        bytes_of(0, half).wait_recv()
        transform(half)
        send(1, half)
    for half in range(2):
        bytes_of(1, half).wait_recv()
        for x in range(22 * half, 22 + 23 * half):
            raw[LINE * (x + 1) + 1 : LINE * (x + 1) + 23, :] = modal_in[flat_row(x) : flat_row(x) + 22, :]

    def all_of(number, rows, at):
        return pltpu.make_async_remote_copy(
            src_ref=raw.at[pl.ds(0, rows)], dst_ref=raw.at[pl.ds(0, rows)], send_sem=send_sem.at[number],
            recv_sem=recv_sem.at[number, at], device_id=peers[2], device_id_type=MESH)

    def exchange(number, grid, kind):
        (to_left, to_right, from_right, from_left), lower, upper = kind
        zero = jnp.zeros((4, 128), F32)
        pieces = []
        for step in range(2):
            rows = jnp.where(
                low_side,
                grid[pl.ds(lower[0] + step, COLS, stride=LINE), :],
                grid[pl.ds(upper[0] + step, COLS, stride=LINE), :])
            line[number, step] = rows
            pieces.append(rows)
        for at, column in enumerate((to_left, to_right)):
            corner[number, at] = jnp.concatenate([p[column : column + 2] for p in pieces] + [zero], 0)
        side[number, 0] = grid[LINE * to_left : LINE * to_left + 48, :]
        side[number, 1] = grid[LINE * to_right : LINE * to_right + 48, :]
        sends = (
            (corner.at[number, 0], corner_in.at[number, 0]),
            (corner.at[number, 1], corner_in.at[number, 1]),
            (line.at[number], line_in.at[number]),
            (side.at[number, 0], side_in.at[number, 0]),
            (side.at[number, 1], side_in.at[number, 1]))
        for at, ((source, target), peer) in enumerate(zip(sends, peers, strict=True)):
            pltpu.make_async_remote_copy(
                src_ref=source, dst_ref=target, send_sem=send_sem.at[number],
                recv_sem=recv_sem.at[number, at // 3], device_id=peer, device_id_type=MESH).start()
        all_of(number, 96, 1).wait_recv()
        grid[LINE * from_right : LINE * from_right + 48, :] += side_in[number, 0]
        grid[LINE * from_left : LINE * from_left + 48, :] += side_in[number, 1]
        all_of(number, 112, 0).wait_recv()
        zeros = jnp.zeros((COLS, 128), F32)
        for step in range(2):
            rows = [line_in[number, step]]
            for at, column in enumerate((from_right, from_left)):
                piece = corner_in[number, at, 2 * step : 2 * step + 2, :]
                before = [jnp.zeros((column, 128), F32)] if column else []
                rows.append(jnp.concatenate(
                    before + [piece, jnp.zeros((COLS - 2 - column, 128), F32)], 0))
            added = rows[0] + rows[1] + rows[2]
            where_low = pl.ds(lower[1] + step, COLS, stride=LINE)
            where_up = pl.ds(upper[1] + step, COLS, stride=LINE)
            grid[where_low, :] += jnp.where(low_side, added, zeros)
            grid[where_up, :] += jnp.where(low_side, zeros, added)

    def rows_of(source, f, first, count):
        return jnp.concatenate(
            [jnp.concatenate(
                [source[264 * e + LINE * (first + a) + 8 * f : 264 * e + LINE * (first + a) + 8 * f + 16, :]
                 for a in range(count)], 0) for e in range(ELEMS)], 1)

    def apply(matrix, value):
        high, low = split(value)
        return dot(matrix[0], high) + dot(matrix[0], low) + dot(matrix[1], high)

    def gathered(parts, x, g, first, count):
        found = None
        for e in range(ELEMS):
            a = x - P_SIZE * e - first
            if not 0 <= a < count:
                continue
            for f in range(ROWS_DEV):
                if 0 <= g - f < 2:
                    row = 16 * a + 8 * (g - f)
                    term = parts[f][row : row + 8, 128 * e : 128 * e + 128]
                    found = term if found is None else found + term
        return found

    def solve(source, target):
        parts = []
        for f in range(ROWS_DEV):
            modal = apply(inward.at[f], rows_of(source, f, 0, EXT_POINTS))
            parts.append(apply(outward.at[f], modal * jnp.concatenate([inverse[f]] * ELEMS, 1)))
        for x in range(COLS):
            for g in range(3):
                found = gathered(parts, x, g, 0, EXT_POINTS)
                row = LINE * x + 8 * g
                target[row : row + 8, :] = jnp.zeros((8, 128), F32) if found is None else found

    field[...] = raw[...]
    exchange(0, field, RESIDUAL)
    solve(field, total)
    exchange(1, total, CORRECTION)
    parts = [apply(local.at[f], rows_of(total, f, 1, NODES)) for f in range(ROWS_DEV)]
    for x in range(COLS):
        for g in range(3):
            row = LINE * x + 8 * g
            found = gathered(parts, x, g, 1, NODES)
            if found is None:
                field[row : row + 8, :] = jnp.zeros((8, 128), F32)
                continue
            mass_x = sum(weights[x - P_SIZE * e - 1] * element_width / 2.0
                         for e in range(ELEMS) if 0 <= x - P_SIZE * e - 1 < NODES)
            field[row : row + 8, :] = (
                raw[row : row + 8, :] - found - (mass_shift[g] * np.float32(mass_x)) * total[row : row + 8, :])
    exchange(2, field, RESIDUAL)
    solve(field, fix)
    exchange(3, fix, CORRECTION)
    out_ref[...] = total[...] + fix[...]
    for number in range(4):
        all_of(number, 208, 0).wait_send()
    for stage in range(2):
        for half in range(2):
            bytes_of(stage, half).wait_send()


def place_kernel(grid_ref, out_ref):
    low_side = lax.axis_index("ey") == 0
    for e in range(ELEMS):
        for f in range(ROWS_DEV):
            for a in range(NODES):
                start = LINE * (P_SIZE * e + 1 + a) + P_SIZE * f
                out_ref[pl.ds(96 * a + 2 * e + f, NODES, stride=8), :] = jnp.where(
                    low_side, grid_ref[start : start + NODES, :], grid_ref[start + 1 : start + 1 + NODES, :])


def on_device(stream_speed, normal_speed):
    single, lambdas_x, weights, heights = all_tables()
    vmem = pl.BlockSpec(memory_space=pltpu.VMEM)
    remote = pl.BlockSpec(memory_space=pltpu.HBM)
    tables = {name: jnp.asarray(table) for name, table in single.items()}
    tables["stream"] = stream_speed.reshape(1152, 64)
    tables["normal"] = normal_speed.reshape(1152, 64)
    given = [tables[name] for name in TABLES]
    grid = pltpu.VMEM((GRID, 128), F32)
    flat = pltpu.VMEM((FLAT, 128), F32)
    solved = pl.pallas_call(
        functools.partial(step_kernel, lambdas_x, weights, heights),
        out_shape=jax.ShapeDtypeStruct((GRID, 128), F32),
        in_specs=[remote] * len(TABLES),
        out_specs=vmem,
        scratch_shapes=[pltpu.VMEM(table.shape, table.dtype) for table in given] + [
            flat, flat, flat, flat,
            pltpu.VMEM((32, 16, 128), F32),
            pltpu.VMEM((4096, 32), F32),
            pltpu.VMEM((16, 128, 256), BF16),
            pltpu.VMEM((2, 2, EXT_POINTS * 16, EXT_POINTS * 16), BF16),
            pltpu.VMEM((2, 2, EXT_POINTS * 16, EXT_POINTS * 16), BF16),
            pltpu.VMEM((2, 2, NODES * 16, NODES * 16), BF16),
            pltpu.VMEM((2, EXT_POINTS * 16, 128), F32),
            grid, grid, grid, grid,
            pltpu.VMEM((4, 2, 48, 128), F32),
            pltpu.VMEM((4, 2, COLS, 128), F32),
            pltpu.VMEM((4, 2, 8, 128), F32),
            pltpu.VMEM((4, 2, 48, 128), F32),
            pltpu.VMEM((4, 2, COLS, 128), F32),
            pltpu.VMEM((4, 2, 8, 128), F32),
            pltpu.SemaphoreType.DMA((len(TABLES),)),
            pltpu.SemaphoreType.DMA((4,)),
            pltpu.SemaphoreType.DMA((4,)),
            pltpu.SemaphoreType.DMA((4,)),
            pltpu.SemaphoreType.DMA((4, 2)),
        ],
        compiler_params=pltpu.CompilerParams(
            collective_id=1, has_side_effects=True, vmem_limit_bytes=54500 * 1024),
        name="step",
    )(*given)
    placed = pl.pallas_call(
        place_kernel,
        out_shape=jax.ShapeDtypeStruct((1152, 128), F32),
        in_specs=[vmem],
        out_specs=vmem,
        compiler_params=pltpu.CompilerParams(vmem_limit_bytes=8 * 2**20),
        name="place",
    )(solved)
    return placed.reshape(12, 12, 4, 2, 128)


def solution(mesh):
    return jax.shard_map(
        on_device,
        mesh=mesh,
        in_specs=(P(None, None, "ex", "ey", "mode"), P(None, None, "ex", "ey", "mode")),
        out_specs=P(None, None, "ex", "ey", "mode"),
        check_vma=False,
    )
```

```python
import functools
import math

import jax
import jax.numpy as jnp
import numpy as np
from jax import lax
from jax.experimental import pallas as pl
from jax.experimental.pallas import tpu as pltpu
from jax.sharding import PartitionSpec as P

P_SIZE = 11
NODES = P_SIZE + 1
FINE = 18
FINE_PAD = 336
ELEMS = 4
ROWS_DEV = 2
ROWS_TOTAL = 4
PLANES = 2048
RANKS = 32
LINE = 24
COLS = 48
GRID = COLS * LINE
FLAT = 1024
EXT_POINTS = NODES + 2
OWN = NODES * LINE

MESH = pl.DeviceIdType.MESH
F32 = jnp.float32
BF16 = jnp.bfloat16

element_width = 2.0
shift_base = 10.0
span_rate = 0.0125


def legendre_pair(degree, points):
    before = points * 0.0 + 1.0
    current = points.copy()
    for step in range(1, degree):
        upcoming = ((2 * step + 1) * points * current - step * before) / (step + 1)
        before = current
        current = upcoming
    return (current, before)


def legendre_slope(degree, points):
    current, before = legendre_pair(degree, points)
    return (current, degree * (points * current - before) / (points * points - 1.0))


def lobatto_points(order):
    guesses = -np.cos(np.pi * np.arange(1, order) / order)
    for step in range(60):
        current, slope = legendre_slope(order, guesses)
        second = (2.0 * guesses * slope - order * (order + 1) * current) / (1.0 - guesses * guesses)
        guesses = guesses - slope / second
    return guesses


def gauss_rule(count):
    guesses = -np.cos(np.pi * (np.arange(count) + 0.75) / (count + 0.5))
    for step in range(60):
        current, slope = legendre_slope(count, guesses)
        guesses = guesses - current / slope
    current, slope = legendre_slope(count, guesses)
    return (guesses, 2.0 / ((1.0 - guesses * guesses) * slope * slope))


def jacobi_eigen(matrix):
    size_n = matrix.shape[0]
    work = matrix.copy()
    vectors = np.eye(size_n)
    for sweep_number in range(20):
        for first in range(size_n):
            for second in range(first + 1, size_n):
                coupling = work[first, second]
                if abs(coupling) > 1e-300:
                    theta = (work[second, second] - work[first, first]) / (2.0 * coupling)
                    direction = 1.0 if theta >= 0.0 else -1.0
                    tangent = direction / (abs(theta) + np.sqrt(theta * theta + 1.0))
                    cosine = 1.0 / np.sqrt(tangent * tangent + 1.0)
                    sine = tangent * cosine
                    rotation = np.eye(size_n)
                    rotation[first, first] = cosine
                    rotation[second, second] = cosine
                    rotation[first, second] = sine
                    rotation[second, first] = -sine
                    work = rotation.T @ work @ rotation
                    vectors = vectors @ rotation
    diagonal_index = np.arange(size_n)
    return (work[diagonal_index, diagonal_index], vectors)


def extended_basis(stiffness, weights, left_width, centre_width, right_width):
    node_count = weights.shape[0]
    full_count = 3 * node_count - 2
    stiff_full = np.zeros((full_count, full_count))
    mass_full = np.zeros(full_count)
    for position, span_width in enumerate((left_width, centre_width, right_width)):
        if span_width > 0.0:
            first_node = position * (node_count - 1)
            stiff_full[
                first_node : first_node + node_count, first_node : first_node + node_count
            ] += stiffness * (2.0 / span_width)
            mass_full[first_node : first_node + node_count] += weights * (span_width / 2.0)
    low_index = node_count - 2
    high_index = low_index + node_count + 2
    stiff_ext = stiff_full[low_index:high_index, low_index:high_index].copy()
    mass_ext = mass_full[low_index:high_index].copy()
    frozen_list = []
    if left_width <= 0.0:
        frozen_list += [0, 1]
    if right_width <= 0.0:
        frozen_list += [node_count, node_count + 1]
    for frozen_index in frozen_list:
        stiff_ext[frozen_index, :] = 0.0
        stiff_ext[:, frozen_index] = 0.0
        stiff_ext[frozen_index, frozen_index] = 1.0
        mass_ext[frozen_index] = 1.0
    inverse_root = 1.0 / np.sqrt(mass_ext)
    lambdas, vectors = jacobi_eigen(inverse_root[:, None] * stiff_ext * inverse_root[None, :])
    return (inverse_root[:, None] * vectors, lambdas)


def spectral_tables(order, rows_total):
    inner_points = lobatto_points(order)
    points = np.concatenate([[-1.0], inner_points, [1.0]])
    values, unused_before = legendre_pair(order, points)
    weights = 2.0 / (order * (order + 1) * values**2)
    identity = np.eye(order + 1)
    point_gaps = points[:, None] - points[None, :] + identity
    derivative = values[:, None] / (values[None, :] * point_gaps) * (1.0 - identity)
    derivative[0, 0] = -order * (order + 1) / 4.0
    derivative[order, order] = order * (order + 1) / 4.0
    stiffness = derivative.T @ (weights[:, None] * derivative)
    gauss_points, gauss_weights = gauss_rule(3 * (order + 1) // 2)
    offsets = gauss_points[:, None, None] - points[None, None, :]
    numerators = np.prod(np.where(identity[None, :, :] > 0.5, 1.0, offsets), axis=2)
    denominators = np.prod(np.where(identity > 0.5, 1.0, points[:, None] - points[None, :]), axis=1)
    interp = numerators / denominators[None, :]
    heights = 0.6 + 1.4 * np.sin(np.pi * (np.arange(rows_total) + 0.5) / rows_total)
    basis_x, lambdas_x = extended_basis(
        stiffness, weights, element_width, element_width, element_width
    )
    basis_rows = []
    lambda_rows = []
    for row_number in range(rows_total):
        below = heights[row_number - 1] if row_number > 0 else 0.0
        above = heights[row_number + 1] if row_number < rows_total - 1 else 0.0
        basis_one, lambda_one = extended_basis(
            stiffness, weights, below, heights[row_number], above
        )
        basis_rows.append(basis_one)
        lambda_rows.append(lambda_one)
    return (
        derivative,
        interp,
        gauss_weights,
        weights,
        stiffness,
        basis_x,
        lambdas_x,
        np.stack(basis_rows),
        np.stack(lambda_rows),
        heights,
    )


def bf16_pair(table):
    high = np.asarray(table, np.float32).astype(BF16)
    low = (np.asarray(table, np.float64) - high.astype(np.float64)).astype(np.float32)
    return high, low.astype(BF16)


def split(value):
    high = value.astype(BF16)
    return high, (value - high.astype(F32)).astype(BF16)


def dot(left, right):
    return jnp.dot(left, right, preferred_element_type=F32)


def dot_rows(left, right):
    return lax.dot_general(left, right, (((1,), (1,)), ((), ())), preferred_element_type=F32)


SMALL = (("wave", 64, 128), ("twist", 128, 128), ("in_x", 16, 224), ("in_y", 64, 224), ("out_x", 16, 224),
         ("out_y", 64, 224), ("own_kx", 16, 192), ("own_my", 64, 192), ("own_wx", 16, 192), ("own_ky", 64, 192),
         ("mass", 48, 128), ("lam", 64, 128))
SMALL_AT = {entry[0]: sum(other[1] for other in SMALL[:at]) for at, entry in enumerate(SMALL)}
SMALL_WIDTH = {name: width for name, _, width in SMALL}


@functools.cache
def all_tables():
    (derivative, interp, gauss_weights, weights, stiffness, basis_x, lambdas_x, basis_y,
     lambdas_y, heights) = spectral_tables(P_SIZE, ROWS_TOTAL)
    nodes = NODES * NODES
    fine = FINE * FINE
    lift = np.zeros((3, FINE_PAD, nodes))
    lift[0, :fine] = np.kron(interp, interp)
    lift[1, :fine] = np.kron(interp @ derivative * (2.0 / element_width), interp)
    lift[2, :fine] = np.kron(interp, interp @ derivative)
    lift = lift.reshape(3 * FINE_PAD, nodes)
    lift_high, lift_low = bf16_pair(lift)
    lift_cat = np.concatenate([lift_high, lift_high, lift_low], 1)
    back = np.zeros((ROWS_DEV, NODES, 16, FINE_PAD))
    quad = np.kron(gauss_weights, gauss_weights)
    back_one = -(np.kron(interp.T, interp.T) * quad[None, :]).reshape(NODES, NODES, fine)
    for f in range(ROWS_DEV):
        back[f, :, 3 * f : 3 * f + NODES, :fine] = back_one
    back_high, back_low = bf16_pair(back.reshape(ROWS_DEV, NODES * 16, FINE_PAD))
    back_cat = np.concatenate([back_high, back_high, back_low], 2)
    plane = np.arange(64)[None, :]
    angle = 2.0 * np.pi * ((np.arange(32)[:, None] * plane) % 64) / 64.0
    wave = np.tile(np.stack([np.cos(angle), np.sin(angle)]), (1, 1, 2))
    twist = np.zeros((16, 4, 2, 2, 64))
    for rp in range(16):
        for half in range(2):
            r = rp if half == 0 else (32 - rp if rp else 16)
            turn = 2.0 * np.pi * r * np.arange(64) / PLANES
            cosine = np.stack([np.cos(turn), -np.sin(turn)]) / PLANES
            sine = np.stack([np.sin(turn), np.cos(turn)]) / PLANES
            if rp == 0:
                twist[rp, 2 * half, :, half] = cosine
                twist[rp, 2 * half + 1, :, half] = -sine
            else:
                sign = 1.0 if half == 0 else -1.0
                twist[rp, 2 * half, :, 0] = cosine
                twist[rp, 2 * half, :, 1] = sign * sine
                twist[rp, 2 * half + 1, :, 0] = -sine
                twist[rp, 2 * half + 1, :, 1] = sign * cosine
    twist = twist.reshape(16, 8, 128)
    line_basis = np.zeros((2, ROWS_DEV, 16, 16))
    line_lambda = np.ones((2, ROWS_DEV, 16))
    line_mass = np.zeros((2, LINE))
    row_mass = np.zeros((2, ROWS_DEV, 16))
    row_stiff = np.zeros((2, ROWS_DEV, 16, 16))
    top = P_SIZE * ROWS_TOTAL
    for ey in range(2):
        for f in range(ROWS_DEV):
            low = 21 * ey + 8 * f
            row = ROWS_DEV * ey + f
            line_lambda[ey, f, :EXT_POINTS] = lambdas_y[row]
            for b in range(EXT_POINTS):
                g = P_SIZE * row + b - 1
                if 0 < g < top:
                    line_basis[ey, f, g - low, :EXT_POINTS] = basis_y[row, b]
            for b in range(NODES):
                g = P_SIZE * row + b
                if 0 < g < top:
                    line_mass[ey, g - 21 * ey] += heights[row] / 2.0 * weights[b]
                    row_mass[ey, f, g - low] = heights[row] / 2.0 * weights[b]
                    for c in range(NODES):
                        h = P_SIZE * row + c
                        if 0 < h < top:
                            row_stiff[ey, f, g - low, h - low] = 2.0 / heights[row] * stiffness[b, c]
    ones_line = np.ones((1, 16))
    in_x = np.kron(basis_x.T, ones_line)
    in_y = np.tile(np.transpose(line_basis, (0, 1, 3, 2)), (1, 1, 1, EXT_POINTS))
    out_x = np.kron(basis_x, ones_line)
    out_y = np.tile(line_basis, (1, 1, 1, EXT_POINTS))
    own_kx = np.kron(stiffness * (2.0 / element_width), ones_line)
    own_my = np.tile(row_mass[..., None] * np.eye(16), (1, 1, 1, NODES))
    own_wx = np.kron(np.diag(weights) * (element_width / 2.0), ones_line)
    own_ky = np.tile(row_stiff, (1, 1, 1, NODES))
    wide = np.ones((1, 1, 128))
    named = dict(
        wave=wave, twist=twist, in_x=in_x, in_y=in_y, out_x=out_x, out_y=out_y, own_kx=own_kx, own_my=own_my,
        own_wx=own_wx, own_ky=own_ky, mass=line_mass[:, :, None] * wide, lam=line_lambda[..., None] * wide[None])
    small = np.zeros((sum(rows for _, rows, _ in SMALL), 256), np.float32)
    for name, rows, width in SMALL:
        table = named[name].reshape(-1, width)
        small[SMALL_AT[name] : SMALL_AT[name] + table.shape[0], :width] = table
    single = dict(lift=lift_cat, back=back_cat, small=small)
    return single, np.asarray(lambdas_x), np.asarray(weights), np.asarray(heights)


def real_transform(values):
    count = len(values)
    if count == 1:
        return [(values[0], None)]
    if count == 2:
        return [(values[0] + values[1], None), (values[0] - values[1], None)]
    even, odd = real_transform(values[0::2]), real_transform(values[1::2])
    quarter, half = count // 4, count // 2
    result = []
    for r in range(half + 1):
        s = r % half

        def pick(part):
            if s <= quarter:
                return part[s], 1.0
            return part[half - s], -1.0

        (er, ei), es = pick(even)
        (dr, di), ds = pick(odd)
        c, n = math.cos(2 * math.pi * r / count), -math.sin(2 * math.pi * r / count)
        if r == 0:
            result.append((er + dr, None))
        elif r == half:
            result.append((er - dr, None))
        elif 4 * r == count:
            result.append((er, -dr))
        else:
            c, n = np.float32(c), np.float32(n)
            if di is None:
                tr, ti = dr * c, dr * n
            else:
                tr = dr * c - di * (n * np.float32(ds))
                ti = dr * n + di * (c * np.float32(ds))
            result.append((er + tr, ti if ei is None else (ti + ei if es > 0 else ti - ei)))
    return result


def flat_row(x):
    return 22 * x if x < 22 else FLAT // 2 + 22 * (x - 22)


RESIDUAL = ((1, 44, 45, 0), (21, 22), (1, 0))
CORRECTION = ((0, 45, 44, 1), (22, 21), (0, 1))
TABLES = ("stream", "normal", "lift", "back", "small")


def step_kernel(lambdas_x, weights, heights, *refs):
    count = len(TABLES)
    sources, out_ref, refs = refs[:count], refs[count], refs[count + 1 :]
    held, refs = dict(zip(TABLES, refs[:count], strict=True)), refs[count:]
    (weak_out, weak_in, modal_out, modal_in, mid_ref, turn_ref, fourier, inward, outward, local, inverse,
     raw, field, fix, total, side, line, corner, side_in, line_in, corner_in,
     table_sem, share_send, share_recv, send_sem, recv_sem) = refs
    me = lax.axis_index("mode")
    ey = lax.axis_index("ey")
    ex = lax.axis_index("ex")
    low_side = ey == 0
    my_z, my_y, my_c = me // 8, lax.rem(me // 2, 4), lax.rem(me, 2)

    z_part = [8 * lax.rem(my_z + dz, 4) for dz in range(4)]
    yc_part = [2 * lax.rem(my_y + group // 2, 4) + lax.rem(my_c + group % 2, 2) for group in range(8)]

    def rank(dz, group):
        return z_part[dz] + yc_part[group]

    def each_rank(act):
        for group in (4, 5, 6, 7, 2, 3, 1, 0):
            for dz in (2, 1, 3):
                act(dz, group)
        for group in (4, 5, 6, 7, 2, 3, 1):
            act(0, group)

    loads = [pltpu.make_async_copy(source, held[name], table_sem.at[at])
             for at, (name, source) in enumerate(zip(TABLES, sources, strict=True))]
    for load in loads[:3]:
        load.start()
    u_ref, v_ref, lift_ref = held["stream"], held["normal"], held["lift"]

    left, right, other = lax.rem(ex + 3, 4), lax.rem(ex + 1, 4), 1 - ey
    peers = ({"ex": left, "ey": other}, {"ex": right, "ey": other}, {"ey": other}, {"ex": left}, {"ex": right})
    barrier = pltpu.get_barrier_semaphore()
    each_rank(lambda dz, group: pl.semaphore_signal(
        barrier, inc=1, device_id={"mode": rank(dz, group)}, device_id_type=MESH))
    for peer in peers:
        pl.semaphore_signal(barrier, inc=1, device_id=peer, device_id_type=MESH)
    for load in loads[3:]:
        load.start()
    for load in loads[:3]:
        load.wait()

    def advect(half):
        first = lax.broadcasted_iota(jnp.int32, (FINE_PAD, 128), 1) < 64
        columns = []
        for f in range(ROWS_DEV):
            for e in (2 * half, 2 * half + 1):
                rows = pl.ds(ROWS_DEV * e + f, NODES * NODES, stride=ROWS_DEV * ELEMS)
                columns.append(jnp.concatenate([u_ref[rows, :], v_ref[rows, :]], 1))
        high, low = split(jnp.concatenate(columns, 1))
        fine = dot(lift_ref[...], jnp.concatenate([high, low, high], 0))
        weak = []
        for f in range(ROWS_DEV):
            half_height = jnp.where(
                low_side, np.float32(heights[f] / 2.0), np.float32(heights[ROWS_DEV + f] / 2.0))
            parts = []
            for e in range(2):
                start = 256 * f + 128 * e
                block = slice(start, start + 128)
                speed = fine[:FINE_PAD, block]
                turned = pltpu.roll(speed, 64, 1)
                along = jnp.where(first, speed, turned) * half_height
                across = jnp.where(first, turned, speed)
                parts.append(
                    along * fine[FINE_PAD : 2 * FINE_PAD, block] + across * fine[2 * FINE_PAD :, block])
            high, low = split(jnp.concatenate(parts, 1))
            if half == 0 and f == 0:
                loads[3].wait()
            weak.append(dot(held["back"][f], jnp.concatenate([high, low, high], 0)))
        lines = []
        for a in range(NODES):
            low_row, high_row = slice(16 * a, 16 * a + 8), slice(16 * a + 8, 16 * a + 16)
            lines += [weak[0][low_row], weak[0][high_row] + weak[1][low_row], weak[1][high_row]]
        weak = jnp.concatenate(lines, 0)
        return jnp.where(low_side, pltpu.roll(weak, OWN - 1, 0), weak)

    def store_weak(half, weak, carried):
        for e in range(2):
            for a in range(NODES):
                x = P_SIZE * (2 * half + e) + a
                if a == P_SIZE and x < 44:
                    continue
                value = weak[LINE * a : LINE * a + 22, 128 * e : 128 * e + 128]
                if a == 0 and e == 1:
                    value += weak[LINE * P_SIZE : LINE * P_SIZE + 22, :128]
                if a == 0 and e == 0 and half == 1:
                    value += carried
                weak_out[flat_row(x) : flat_row(x) + 22, :] = value
        spare = (484, 512) if half == 0 else (1018, 1024)
        weak_out[spare[0] : spare[1], :] = jnp.zeros((spare[1] - spare[0], 128), F32)
        return weak[LINE * P_SIZE : LINE * P_SIZE + 22, 128:]

    def send(stage, half):
        source, target = ((weak_out, weak_in), (modal_out, modal_in))[stage]
        base, number = FLAT // 2 * half, 2 * stage + half
        mine = pl.ds(pl.multiple_of(base + 16 * me, 16), 16)

        def start(dz, group):
            peer = rank(dz, group)
            pltpu.make_async_remote_copy(
                src_ref=source.at[pl.ds(pl.multiple_of(base + 16 * peer, 16), 16)],
                dst_ref=target.at[mine],
                send_sem=share_send.at[number],
                recv_sem=share_recv.at[number],
                device_id={"mode": peer},
                device_id_type=MESH,
            ).start()

        each_rank(start)
        target[mine, :] = source[mine, :]

    def bytes_of(stage, half):
        source, target = ((weak_out, weak_in), (modal_out, modal_in))[stage]
        rows, number = pl.ds(0, 16 * (RANKS - 1)), 2 * stage + half
        return pltpu.make_async_remote_copy(
            src_ref=source.at[rows], dst_ref=target.at[rows], send_sem=share_send.at[number],
            recv_sem=share_recv.at[number], device_id={"mode": rank(2, 0)}, device_id_type=MESH)

    def transform(half):
        base = FLAT // 2 * half
        for block in range(2):
            rows = slice(8 * block, 8 * block + 8)
            starts = [base + 16 * d + 8 * block for d in range(RANKS)]
            found = real_transform([weak_in[s : s + 8, :] for s in starts])
            for r in range(1, 16):
                mid_ref[2 * r, rows, :], mid_ref[2 * r + 1, rows, :] = found[r]
            mid_ref[0, rows, :] = found[0][0]
            mid_ref[1, rows, :] = found[16][0]
        first = lax.broadcasted_iota(jnp.int32, (16, 128), 1) < 64
        for rp in range(16):
            real, imag = mid_ref[2 * rp], mid_ref[2 * rp + 1]
            both = jnp.concatenate(
                [jnp.where(first, real, pltpu.roll(imag, 64, 1)),
                 jnp.where(first, pltpu.roll(real, 64, 1), imag)], 0)
            high, low = split(both)
            table = fourier[rp]
            found = dot_rows(table, jnp.concatenate([high, high], 1)) + dot_rows(table[:, :128], low)
            for at in range(2):
                r = rp if at == 0 else (32 - rp if rp else 16)
                for c in range(2):
                    start = 32 * (2 * at + c)
                    for k in range(2):
                        turn_ref[pl.ds(4 * r + 2 * c + k, 32, stride=128), :] = found[start : start + 32, :]
        even = lax.broadcasted_iota(jnp.int32, (16, 128), 1) % 2 == 0
        for q in range(RANKS):
            turned = turn_ref[128 * q : 128 * q + 128, :].T
            modal_out[base + 16 * q : base + 16 * q + 16, :] = jnp.where(even, turned[:16], turned[16:])

    carried = store_weak(0, advect(0), None)
    pl.semaphore_wait(barrier, RANKS - 1 + 5)
    send(0, 0)
    store_weak(1, advect(1), carried)
    send(0, 1)

    def part(name, start, count):
        return held["small"][pl.ds(SMALL_AT[name] + start, count), : SMALL_WIDTH[name]]

    def row_part(name, f):
        start = pl.multiple_of(SMALL_AT[name] + 16 * (ROWS_DEV * ey + f), 16)
        return held["small"][pl.ds(start, 16), : SMALL_WIDTH[name]]

    for load in loads[4:]:
        load.wait()
    for rp in range(16):
        for at in range(4):
            pair = part("twist", 8 * rp + 2 * at, 2)
            high, low = split(part("wave", 0, 32) * pair[:1] + part("wave", 32, 32) * pair[1:])
            fourier[rp, 32 * at : 32 * at + 32, :128] = high
            fourier[rp, 32 * at : 32 * at + 32, 128:] = low
    lane = lax.broadcasted_iota(jnp.int32, (1, 128), 1)
    mode = (me * 32 + lane // 4).astype(F32)
    shift = shift_base + (np.float32(span_rate) * mode) ** 2
    for f in range(ROWS_DEV):
        for i in range(EXT_POINTS):
            rows = slice(16 * i, 16 * i + 16)
            high, low = split(part("in_x", i, 1) * row_part("in_y", f))
            inward[f, 0, rows, :], inward[f, 1, rows, :] = high, low
            high, low = split(part("out_x", i, 1) * row_part("out_y", f))
            outward[f, 0, rows, :], outward[f, 1, rows, :] = high, low
            inverse[f, rows, :] = 1.0 / (row_part("lam", f) + (shift + np.float32(lambdas_x[i])))
        for a in range(NODES):
            rows = slice(16 * a, 16 * a + 16)
            high, low = split(
                part("own_kx", a, 1) * row_part("own_my", f)
                + part("own_wx", a, 1) * row_part("own_ky", f))
            local[f, 0, rows, :], local[f, 1, rows, :] = high, low
    mass_shift = [held["small"][pl.ds(pl.multiple_of(SMALL_AT["mass"] + LINE * ey + 8 * g, 8), 8), :128] * shift for g in range(3)]
    raw[...] = jnp.zeros((GRID, 128), F32)

    for half in range(2):
        bytes_of(0, half).wait_recv()
        transform(half)
        send(1, half)
    for half in range(2):
        bytes_of(1, half).wait_recv()
        for x in range(22 * half, 22 + 23 * half):
            raw[LINE * (x + 1) + 1 : LINE * (x + 1) + 23, :] = modal_in[flat_row(x) : flat_row(x) + 22, :]

    def all_of(number, rows, at):
        return pltpu.make_async_remote_copy(
            src_ref=raw.at[pl.ds(0, rows)], dst_ref=raw.at[pl.ds(0, rows)], send_sem=send_sem.at[number],
            recv_sem=recv_sem.at[number, at], device_id=peers[2], device_id_type=MESH)

    def exchange(number, grid, kind, landing=None, meanwhile=None):
        (to_left, to_right, from_right, from_left), lower, upper = kind
        zero = jnp.zeros((4, 128), F32)
        pieces = []
        for step in range(2):
            rows = jnp.where(
                low_side,
                grid[pl.ds(lower[0] + step, COLS, stride=LINE), :],
                grid[pl.ds(upper[0] + step, COLS, stride=LINE), :])
            line[number, step] = rows
            pieces.append(rows)
        for at, column in enumerate((to_left, to_right)):
            corner[number, at] = jnp.concatenate([p[column : column + 2] for p in pieces] + [zero], 0)
        side[number, 0] = grid[LINE * to_left : LINE * to_left + 48, :]
        side[number, 1] = grid[LINE * to_right : LINE * to_right + 48, :]
        sends = (
            (corner.at[number, 0], corner_in.at[number, 0]),
            (corner.at[number, 1], corner_in.at[number, 1]),
            (line.at[number], line_in.at[number]),
            (side.at[number, 0], side_in.at[number, 0]),
            (side.at[number, 1], side_in.at[number, 1]))
        for at, ((source, target), peer) in enumerate(zip(sends, peers, strict=True)):
            pltpu.make_async_remote_copy(
                src_ref=source, dst_ref=target, send_sem=send_sem.at[number],
                recv_sem=recv_sem.at[number, at // 3], device_id=peer, device_id_type=MESH).start()
        if landing is None:
            landing = grid
        if meanwhile is not None:
            meanwhile()
        all_of(number, 96, 1).wait_recv()
        landing[LINE * from_right : LINE * from_right + 48, :] += side_in[number, 0]
        landing[LINE * from_left : LINE * from_left + 48, :] += side_in[number, 1]
        all_of(number, 112, 0).wait_recv()
        zeros = jnp.zeros((COLS, 128), F32)
        for step in range(2):
            rows = [line_in[number, step]]
            for at, column in enumerate((from_right, from_left)):
                piece = corner_in[number, at, 2 * step : 2 * step + 2, :]
                before = [jnp.zeros((column, 128), F32)] if column else []
                rows.append(jnp.concatenate(
                    before + [piece, jnp.zeros((COLS - 2 - column, 128), F32)], 0))
            added = rows[0] + rows[1] + rows[2]
            where_low = pl.ds(lower[1] + step, COLS, stride=LINE)
            where_up = pl.ds(upper[1] + step, COLS, stride=LINE)
            landing[where_low, :] += jnp.where(low_side, added, zeros)
            landing[where_up, :] += jnp.where(low_side, zeros, added)

    def rows_of(source, f, first, count):
        return jnp.concatenate(
            [jnp.concatenate(
                [source[264 * e + LINE * (first + a) + 8 * f : 264 * e + LINE * (first + a) + 8 * f + 16, :]
                 for a in range(count)], 0) for e in range(ELEMS)], 1)

    def apply(matrix, value):
        high, low = split(value)
        return dot(matrix[0], high) + dot(matrix[0], low) + dot(matrix[1], high)

    def gathered(parts, x, g, first, count):
        found = None
        for e in range(ELEMS):
            a = x - P_SIZE * e - first
            if not 0 <= a < count:
                continue
            for f in range(ROWS_DEV):
                if 0 <= g - f < 2:
                    row = 16 * a + 8 * (g - f)
                    term = parts[f][row : row + 8, 128 * e : 128 * e + 128]
                    found = term if found is None else found + term
        return found

    def solve(source, target):
        parts = []
        for f in range(ROWS_DEV):
            modal = apply(inward.at[f], rows_of(source, f, 0, EXT_POINTS))
            parts.append(apply(outward.at[f], modal * jnp.concatenate([inverse[f]] * ELEMS, 1)))
        for x in range(COLS):
            for g in range(3):
                found = gathered(parts, x, g, 0, EXT_POINTS)
                row = LINE * x + 8 * g
                target[row : row + 8, :] = jnp.zeros((8, 128), F32) if found is None else found

    def copy_raw():
        field[...] = raw[...]

    def add_up():
        out_ref[...] = total[...] + fix[...]

    exchange(0, raw, RESIDUAL, field, copy_raw)
    solve(field, total)
    exchange(1, total, CORRECTION)
    parts = [apply(local.at[f], rows_of(total, f, 1, NODES)) for f in range(ROWS_DEV)]
    for x in range(COLS):
        for g in range(3):
            row = LINE * x + 8 * g
            found = gathered(parts, x, g, 1, NODES)
            if found is None:
                field[row : row + 8, :] = jnp.zeros((8, 128), F32)
                continue
            mass_x = sum(weights[x - P_SIZE * e - 1] * element_width / 2.0
                         for e in range(ELEMS) if 0 <= x - P_SIZE * e - 1 < NODES)
            field[row : row + 8, :] = (
                raw[row : row + 8, :] - found - (mass_shift[g] * np.float32(mass_x)) * total[row : row + 8, :])
    exchange(2, field, RESIDUAL)
    solve(field, fix)
    exchange(3, fix, CORRECTION, out_ref, add_up)
    for number in range(4):
        all_of(number, 208, 0).wait_send()
    for stage in range(2):
        for half in range(2):
            bytes_of(stage, half).wait_send()


def place_kernel(grid_ref, out_ref):
    low_side = lax.axis_index("ey") == 0
    for e in range(ELEMS):
        for f in range(ROWS_DEV):
            for a in range(NODES):
                start = LINE * (P_SIZE * e + 1 + a) + P_SIZE * f
                out_ref[pl.ds(96 * a + 2 * e + f, NODES, stride=8), :] = jnp.where(
                    low_side, grid_ref[start : start + NODES, :], grid_ref[start + 1 : start + 1 + NODES, :])


def on_device(stream_speed, normal_speed):
    single, lambdas_x, weights, heights = all_tables()
    vmem = pl.BlockSpec(memory_space=pltpu.VMEM)
    remote = pl.BlockSpec(memory_space=pltpu.HBM)
    tables = {name: jnp.asarray(table) for name, table in single.items()}
    tables["stream"] = stream_speed.reshape(1152, 64)
    tables["normal"] = normal_speed.reshape(1152, 64)
    given = [tables[name] for name in TABLES]
    grid = pltpu.VMEM((GRID, 128), F32)
    flat = pltpu.VMEM((FLAT, 128), F32)
    solved = pl.pallas_call(
        functools.partial(step_kernel, lambdas_x, weights, heights),
        out_shape=jax.ShapeDtypeStruct((GRID, 128), F32),
        in_specs=[remote] * len(TABLES),
        out_specs=vmem,
        scratch_shapes=[pltpu.VMEM(table.shape, table.dtype) for table in given] + [
            flat, flat, flat, flat,
            pltpu.VMEM((32, 16, 128), F32),
            pltpu.VMEM((4096, 32), F32),
            pltpu.VMEM((16, 128, 256), BF16),
            pltpu.VMEM((2, 2, EXT_POINTS * 16, EXT_POINTS * 16), BF16),
            pltpu.VMEM((2, 2, EXT_POINTS * 16, EXT_POINTS * 16), BF16),
            pltpu.VMEM((2, 2, NODES * 16, NODES * 16), BF16),
            pltpu.VMEM((2, EXT_POINTS * 16, 128), F32),
            grid, grid, grid, grid,
            pltpu.VMEM((4, 2, 48, 128), F32),
            pltpu.VMEM((4, 2, COLS, 128), F32),
            pltpu.VMEM((4, 2, 8, 128), F32),
            pltpu.VMEM((4, 2, 48, 128), F32),
            pltpu.VMEM((4, 2, COLS, 128), F32),
            pltpu.VMEM((4, 2, 8, 128), F32),
            pltpu.SemaphoreType.DMA((len(TABLES),)),
            pltpu.SemaphoreType.DMA((4,)),
            pltpu.SemaphoreType.DMA((4,)),
            pltpu.SemaphoreType.DMA((4,)),
            pltpu.SemaphoreType.DMA((4, 2)),
        ],
        compiler_params=pltpu.CompilerParams(
            collective_id=1, has_side_effects=True, vmem_limit_bytes=54500 * 1024),
        name="step",
    )(*given)
    placed = pl.pallas_call(
        place_kernel,
        out_shape=jax.ShapeDtypeStruct((1152, 128), F32),
        in_specs=[vmem],
        out_specs=vmem,
        compiler_params=pltpu.CompilerParams(vmem_limit_bytes=8 * 2**20),
        name="place",
    )(solved)
    return placed.reshape(12, 12, 4, 2, 128)


def solution(mesh):
    return jax.shard_map(
        on_device,
        mesh=mesh,
        in_specs=(P(None, None, "ex", "ey", "mode"), P(None, None, "ex", "ey", "mode")),
        out_specs=P(None, None, "ex", "ey", "mode"),
        check_vma=False,
    )
```
